32 devices in a mesh: grp: 2 (over y), gx: 4 (over z), gy: 2 (over x), row: 2 (over core).
Axes of the slice: x: 2, y: 2, z: 4, core: 2. Of those that a mesh axis runs over, the one named last changes fastest.
Arguments:
- conc: float32 [64, 8, 16, 128], P(None, ('grp', 'gx'), ('gy', 'row')), parts along dimension 1, may hold values from 0.2 to 2
- cotangent: float32 [64, 8, 16, 128], P(None, ('grp', 'gx'), ('gy', 'row')), parts along dimension 1, may hold values from -6 to 6
- courant: float32 [32, 128], P(('grp', 'gy', 'row')), parts along dimension 0, may hold values from 8 to 100
- direction: int32 [32, 128], P(('grp', 'gy', 'row')), parts along dimension 0, may hold values 0 or 1
- rate_const: float32 [1024], replicated, may hold values from 0.01 to 0.1
- orders: int32 [1024, 64], replicated, may hold values from 0 to 2, as said below
- stoich: int32 [64, 1024], replicated, may hold values from -2 to 1, as said below
Outputs:
- final_state: float32 [64, 8, 16, 128], P(None, ('grp', 'gx'), ('gy', 'row')), parts along dimension 1
- adjoint: float32 [64, 8, 16, 128], P(None, ('grp', 'gx'), ('gy', 'row')), parts along dimension 1
The draws below stay inside these ranges and needn't reach their ends.
There are 2 independent parts, one for each index of `grp`. The reference program is written for one: setup_inputs(seed, part) draws one part's arguments, and reference() takes and returns one part's arrays. A program takes and returns all parts, laid end to end along the dimension named above; an argument that names none is the same for every part. Nothing has to cross between parts.
Inputs may be any that keep to these rules, and one draw needn't show every extreme that they name: `orders`: each reaction has two different reactants, each of order 1 or 2, and no other nonzero order. stoich[s, j] is 1 for the product species of reaction j (one species) minus orders[j, s].
All inputs are finite; a program needn't handle non-finite values. No bound on the sum of `direction` on one device may be relied on, other than what follows from the above.
Results may differ from the reference program's by a relative error of at most 0.0003.
Values sent between devices are 32-bit elements; how exact they have to be, the bound alone decides.
A program may use at most 64 MiB of HBM per device.

```python
import math
import jax
import jax.numpy as jnp
from jax import lax

S = 64
R = 1024
NZ = 128
STEPS = 2
NX = 4
NY = 16


def reaction_table(key):
    base = jax.random.fold_in(key, 11)
    key_one, key_two, key_three, key_four, key_five = jax.random.split(base, 5)
    reactant_one = jax.random.randint(key_one, (R,), 0, S)
    reactant_two = (reactant_one + jax.random.randint(key_two, (R,), 1, S)) % S
    product = jax.random.randint(key_three, (R,), 0, S)
    order_one = jax.random.randint(key_four, (R,), 1, 3)
    order_two = jax.random.randint(key_five, (R,), 1, 3)
    species = jnp.arange(S, dtype=jnp.int32)[None, :]
    orders = (species == reactant_one[:, None]).astype(jnp.int32) * order_one[:, None]
    orders = orders + (species == reactant_two[:, None]).astype(jnp.int32) * order_two[:, None]
    stoich = (species == product[:, None]).astype(jnp.int32) - orders
    return (orders, stoich.T)


def draw_orders(key, part):
    return reaction_table(key)[0]


def draw_stoich(key, part):
    return reaction_table(key)[1]


def touch_ends(entries, rng, smallest, largest):
    spot = [jax.random.randint(jax.random.fold_in(rng, axis), (), 0, length) for axis, length in enumerate(entries.shape)]
    main_axis = entries.shape.index(max(entries.shape))
    beside = spot[:main_axis] + [(spot[main_axis] + 1) % entries.shape[main_axis]] + spot[main_axis + 1:]
    return entries.at[tuple(spot)].set(smallest).at[tuple(beside)].set(largest)


def steps_of(rng, shape, cuts, least, high):
    level, own = 1.0, jax.random.fold_in(rng, 6)
    for axis_at, shards_of in cuts:
        heights = jnp.exp(jax.random.uniform(jax.random.fold_in(own, axis_at), (shards_of,), jnp.float32, least / len(cuts), high / len(cuts)))
        level = level * jnp.repeat(heights, shape[axis_at] // shards_of).reshape([-1 if axis == axis_at else 1 for axis in range(len(shape))])
    return level


def gaussian(key, dims, width, bound, cuts=(), kind=jnp.bfloat16):
    loudness = steps_of(key, dims, cuts, -0.22, 0.18) if cuts else 1.0
    entries = jax.random.normal(key, dims, jnp.float32) * width * loudness
    return jnp.minimum(jnp.maximum(entries, -bound), bound).astype(kind)


def setup_inputs(seed: int = 0, part: int = 0) -> dict:
    key_list = jax.random.split(jax.random.key(seed), 8)
    part_keys = jax.random.split(jax.random.fold_in(key_list[7], part), 8)
    conc = jnp.clip(0.2 + 1.8 * jax.random.uniform(part_keys[0], (S, NX, NY, NZ), jnp.float32) ** steps_of(part_keys[0], (S, NX, NY, NZ), ((1, 4), (2, 4)), -0.2, 0.2), 0.2, 2.0)
    cotangent = gaussian(part_keys[1], (S, NX, NY, NZ), 1.0, 6.0, ((1, 4), (2, 4)), jnp.float32)
    courant = jnp.clip(jnp.exp(math.log(100.0) - 2.5257286 * jax.random.uniform(part_keys[2], (NY, NZ), jnp.float32) ** steps_of(part_keys[2], (NY, NZ), ((0, 4),), -0.2, 0.2)), 8.0, 100.0)
    direction = touch_ends((jax.random.randint(part_keys[3], (NY, NZ), 0, 2) < 1).astype(jnp.int32), jax.random.fold_in(part_keys[3], 1), 0, 1)
    rate_const = jnp.clip(jnp.exp(jax.random.uniform(key_list[4], (R,), jnp.float32, math.log(0.01), math.log(0.1))), 0.01, 0.1)
    orders = draw_orders(jax.random.fold_in(key_list[7], 71), part)
    stoich = draw_stoich(jax.random.fold_in(key_list[7], 71), part)
    return dict(conc=conc, cotangent=cotangent, courant=courant, direction=direction, rate_const=rate_const, orders=orders, stoich=stoich)


time_step = 0.1
diffusion = 0.1
highest = lax.Precision.HIGHEST


def combine_pairs(leading, trailing):
    return (leading[0] * trailing[0], trailing[0] * leading[1] + trailing[1])


def recurrence(values, weight, backward):
    multipliers = jnp.broadcast_to(weight[None, None], (1, values.shape[1]) + weight.shape)
    return lax.associative_scan(combine_pairs, (multipliers, values), reverse=backward, axis=1)


def sweep(values, weight, upward):
    rising = recurrence(values, weight, False)[1]
    falling = recurrence(values, weight, True)[1]
    return jnp.where(upward[None, None], rising, falling)


def smooth(values):
    padded = jnp.pad(values, ((0, 0), (0, 0), (1, 1), (1, 1)))
    beside_all = padded[:, :, 2:, 1:-1] + padded[:, :, :-2, 1:-1] + padded[:, :, 1:-1, 2:] + padded[:, :, 1:-1, :-2]
    return values + diffusion * (beside_all - 4.0 * values)


def to_slices(values):
    return jnp.moveaxis(values.reshape(values.shape[0], values.shape[1], -1), 1, 0)


def from_slices(slices, shape):
    return jnp.moveaxis(slices, 0, 1).reshape(shape)


def reaction_rates(cells, order_float, rate_const):
    activity = 0.5 * jnp.log1p(cells * cells)
    return rate_const[:, None] * jnp.exp(jnp.dot(order_float, activity, precision=highest))


def reference(conc, cotangent, courant, direction, rate_const, orders, stoich):
    order_float = orders.astype(jnp.float32)
    stoich_float = stoich.astype(jnp.float32)
    retain = courant / (1.0 + courant)
    admit = 1.0 / (1.0 + courant)

    def react(cells):
        return cells + time_step * jnp.dot(stoich_float, reaction_rates(cells, order_float, rate_const), precision=highest)

    def react_back(paired):
        cells, spread = paired
        rates = reaction_rates(cells, order_float, rate_const)
        pulled = jnp.dot(stoich_float.T, spread, precision=highest)
        summed = jnp.dot(order_float.T, rates * pulled, precision=highest)
        return spread + time_step * cells / (1.0 + cells * cells) * summed

    states = [conc]
    for position in range(STEPS):
        current = states[-1]
        starred = from_slices(lax.map(react, to_slices(current)), current.shape)
        states.append(sweep(admit * smooth(starred), retain, direction == 1))
    adjoint = cotangent
    for position in reversed(range(STEPS)):
        carried = admit * sweep(adjoint, retain, direction == 0)
        spread = smooth(carried)
        adjoint = from_slices(lax.map(react_back, (to_slices(states[position]), to_slices(spread))), spread.shape)
    return states[-1], adjoint
```

```python
import functools

import jax
import jax.numpy as jnp
from jax import lax
from jax.experimental import pallas as pl
from jax.experimental.pallas import tpu as pltpu
from jax.sharding import PartitionSpec as P

MESH = pl.DeviceIdType.MESH
F32 = jnp.float32
BF16 = jnp.bfloat16
TIME_STEP = 0.1
DIFFUSION = 0.1
HALF_LOG2E = 0.5 * 1.4426950408889634
STAR0, CARRY1, STAR1, CARRY0 = range(4)
DIRECT, RELAY = "direct", "relay"


def plan(kind, nx):
    raw, led = {}, {}
    for q in range(1, nx):
        count = q if kind == DIRECT or q <= 2 else 0
        for k in range(1, count + 1):
            raw.setdefault(k, []).append(q)
        if count < q:
            led.setdefault(count + 1, []).append(q)
    return raw, led


def member(q, places):
    found, places = None, sorted(places)
    while places:
        size = 1
        while size < len(places) and places[size] == places[0] + size:
            size += 1
        run = (q >= places[0]) & (q <= places[size - 1])
        found = run if found is None else found | run
        places = places[size:]
    return found


def kernel(
    sizes, kinds, conc_hbm, cot_hbm, cour_hbm, dir_hbm, const_hbm, ord_hbm, sto_hbm, out_fin, out_adj,
    conc, cot, state, spread, lam, field, sib, mixed, mixed_h, swept, recv, aux_out, aux_in,
    cour_v, dir_v, const_v, rates0, rates1, rates_b, grad_b,
    ord_i, sto_i, ord2, ord_t, sto2, sto, log_k,
    in_sem, tab_sem, send_sem, dsend_sem, recv_sem, lsend_sem, wrecv_sem, esend_sem, erecv_sem,
):
    nx, ngy, nrow = sizes
    depth, species, width = conc.shape
    halo = depth
    reactions = ord_i.shape[1]
    late = [1, 0] if depth > 1 else [0]
    early = [list(range(r, min(r + 2, depth))) for r in range(2, depth, 2)]
    order = [r for rows in early for r in rows] + late + [halo]
    chunk = min(256, reactions)
    plans = [plan(kind, nx) for kind in kinds]
    spans = [max([0, *raw, *led]) for raw, led in plans]

    x = lax.axis_index("gx")
    gy = lax.axis_index("gy")
    row = lax.axis_index("row")
    q_of = [x, nx - 1 - x]
    there = jnp.where(row == 0, gy > 0, gy < ngy - 1)
    across = {"gy": gy + 2 * row - 1, "row": 1 - row}
    beside = {"row": 1 - row}

    def place(r):
        return r + row * (depth - 1 - 2 * r)

    def load(source, target, base):
        return [pltpu.make_async_copy(source.at[:, 0, r, :], target.at[place(r)], in_sem.at[base, r]) for r in range(depth)]

    loads_conc = load(conc_hbm, conc, 0)
    loads_cot = load(cot_hbm, cot, 1)
    tables = [pltpu.make_async_copy(a, b, tab_sem.at[i]) for i, (a, b) in enumerate(
        ((ord_hbm, ord_i), (sto_hbm, sto_i), (const_hbm, const_v), (cour_hbm, cour_v), (dir_hbm, dir_v)))]
    for copy in tables + loads_conc + loads_cot:
        copy.start()

    def inside(target):
        return (target >= 0) & (target < nx)

    own_span, halo_span = max(spans[:depth]), spans[halo]
    partners = [(None, beside)]
    for k in range(1, max(own_span, halo_span) + 1):
        for sign in (1, -1):
            partners.append((inside(x + sign * k), {"gx": x + sign * k}))
    partners.append((there, across))
    for k in range(1, halo_span + 1):
        for sign in (1, -1):
            partners.append((there & inside(x + sign * k), {"gx": x + sign * k, **across}))

    def when(condition, action):
        if condition is None:
            action()
        else:
            pl.when(condition)(action)

    barrier = pltpu.get_barrier_semaphore()
    for condition, device in partners:
        when(condition, lambda: pl.semaphore_signal(barrier, inc=1, device_id=device, device_id_type=MESH))

    def nothing(ref, *index):
        ref[index] = jnp.zeros_like(ref[index])

    for r in range(depth + 1):
        raw, led = plans[r]
        for d in range(2):
            for k in range(1, spans[r] + 1):
                got = member(q_of[d], raw.get(k, []) + led.get(k, []))
                if r == halo:
                    got = got & there

                @pl.when(jnp.logical_not(got))
                def _():
                    for p in range(2):
                        nothing(recv, p, d, r, k - 1)

    @pl.when(jnp.logical_not(there))
    def _():
        nothing(field, STAR0, halo)
        nothing(aux_in, slice(None))
        for p in range(2):
            for d in range(2):
                nothing(mixed_h, p, d)

    for copy in tables:
        copy.wait()

    def pick(ref, r):
        return jnp.where(row == 0, ref[r:r + 1], ref[depth - 1 - r:depth - r])

    courant = [pick(cour_v, r) for r in range(depth)]
    upward = [pick(dir_v, r).astype(F32) for r in range(depth)]
    aux_out[...] = jnp.zeros_like(aux_out)
    aux_out[0:1] = courant[0]
    aux_out[1:2] = upward[0]
    retain = [c / (1.0 + c) for c in courant]
    admit = [1.0 / (1.0 + c) for c in courant]
    rising = [jnp.broadcast_to(u, (species, width)) > 0.5 for u in upward]

    order_float = ord_i[...].astype(F32)
    ord_t[...] = order_float.astype(BF16)
    order_trans = order_float.T.astype(BF16)
    ord2[:, :species] = order_trans
    ord2[:, species:] = order_trans
    stoich_float = sto_i[...].astype(F32)
    sto[...] = stoich_float.astype(BF16)
    stoich_trans = stoich_float.T.astype(BF16)
    sto2[:, :species] = stoich_trans
    sto2[:, species:] = stoich_trans
    log_k[...] = jnp.broadcast_to(jnp.log(const_v[...]) * (2.0 * HALF_LOG2E), (width, reactions)).T
    for copy in loads_conc:
        copy.wait()

    drains = []

    def begin(condition, make):
        when(condition, lambda: make().start())
        drains.append((condition, make))

    def along(p, d, r, k, source, swept_value):
        return pltpu.make_async_remote_copy(
            src_ref=source, dst_ref=recv.at[p, d, r, k - 1],
            send_sem=(lsend_sem if swept_value else send_sem).at[p, d, r, k - 1], recv_sem=recv_sem.at[p, d, r, k - 1],
            device_id={"gx": x + k * (1 - 2 * d)}, device_id_type=MESH)

    def aslant(p, d, k):
        return pltpu.make_async_remote_copy(
            src_ref=mixed.at[p, d, 0], dst_ref=mixed_h.at[p, d] if k == 0 else recv.at[p, d, halo, k - 1],
            send_sem=dsend_sem.at[p, d, k], recv_sem=wrecv_sem.at[p, d] if k == 0 else recv_sem.at[p, d, halo, k - 1],
            device_id={"gx": x + k * (1 - 2 * d), **across} if k else across, device_id_type=MESH)

    def send_raw(p, r):
        for k in sorted(plans[r][0], reverse=True):
            for d in range(2):
                begin(member(q_of[d], [q - k for q in plans[r][0][k]]), functools.partial(along, p, d, r, k, mixed.at[p, d, r], False))

    def send_aslant(p):
        for k in sorted(plans[halo][0], reverse=True):
            for d in range(2):
                begin(there & member(q_of[d], [q - k for q in plans[halo][0][k]]), functools.partial(aslant, p, d, k))
        for d in range(2):
            begin(there, functools.partial(aslant, p, d, 0))

    def arrivals(p, d, r):
        raw, led = plans[r]
        if r == halo:
            yield there, aslant(p, d, 0)
        for k in range(1, spans[r] + 1):
            for table in (raw, led):
                if k in table:
                    got = member(q_of[d], table[k])
                    yield got & there if r == halo and table is raw else got, along(p, d, r, k, recv.at[p, d, r, k - 1], False)

    def passing(d, r):
        return [q - k for k, places in plans[r][1].items() for q in places]

    def total(p, d, r):
        value = mixed_h[p, d] if r == halo else mixed[p, d, r]
        carried = None
        for k in range(spans[r], 0, -1):
            carried = recv[p, d, r, k - 1] if carried is None else recv[p, d, r, k - 1] + retain[r] * carried
        return value if carried is None else value + retain[r] * carried

    def relay(p, r):
        led = plans[r][1]
        for d in range(2):
            if not passing(d, r):
                continue
            @pl.when(member(q_of[d], passing(d, r)))
            def _():
                for got, copy in arrivals(p, d, r):
                    pl.when(got)(copy.wait_recv)
                swept[p, d, r] = total(p, d, r)
            for k, places in led.items():
                begin(member(q_of[d], [q - k for q in places]), functools.partial(along, p, d, r, k, swept.at[p, d, r], True))

    def collect(p, r):
        for d in range(2):
            for got, copy in arrivals(p, d, r):
                if passing(d, r):
                    got = got & jnp.logical_not(member(q_of[d], passing(d, r)))
                pl.when(got)(copy.wait_recv)
        ahead, back = total(p, 0, r), total(p, 1, r)
        return jnp.where(rising[r], ahead, back), jnp.where(rising[r], back, ahead)

    def edge_copy(k):
        if k < 4:
            return pltpu.make_async_remote_copy(
                src_ref=field.at[k, depth - 1], dst_ref=sib.at[k], send_sem=esend_sem.at[k], recv_sem=erecv_sem.at[k],
                device_id=beside, device_id_type=MESH)
        source, target = ((field.at[STAR0, 0], field.at[STAR0, halo]), (aux_out, aux_in))[k - 4]
        return pltpu.make_async_remote_copy(
            src_ref=source, dst_ref=target, send_sem=esend_sem.at[k], recv_sem=erecv_sem.at[k],
            device_id=across, device_id_type=MESH)

    def edge_send(k):
        begin(None if k < 4 else there, functools.partial(edge_copy, k))

    def edge_wait(k):
        when(None if k < 4 else there, lambda: edge_copy(k).wait_recv())

    lane = lax.broadcasted_iota(jnp.int32, (species, width), 1)

    def smooth(k, r):
        here = field[k, r]
        below = field[k, halo] if r == 0 else field[k, r - 1]
        above = sib[k] if r == depth - 1 else field[k, r + 1]
        before = jnp.where(lane == 0, 0.0, pltpu.roll(here, 1, 1))
        after = jnp.where(lane == width - 1, 0.0, pltpu.roll(here, width - 1, 1))
        return here + DIFFUSION * (above + below + after + before - 4.0 * here)

    def side(parts):
        return parts[0] if len(parts) == 1 else jnp.concatenate(parts, axis=1)

    def split(value):
        high = value.astype(BF16)
        low = (value - high.astype(F32)).astype(BF16)
        return jnp.concatenate([high, low], axis=0)

    parts = [pl.ds(i, chunk) for i in range(0, reactions, chunk)]

    def keep(target, part, cols, value):
        high = value.astype(BF16)
        target[0, part, cols] = high
        target[1, part, cols] = (value - high.astype(F32)).astype(BF16)

    def gather(table, halves, cols):
        small = jnp.dot(table[...], halves[1, :, cols], preferred_element_type=F32)
        return small + jnp.dot(table[...], halves[0, :, cols], preferred_element_type=F32)

    def columns(rows):
        return pl.ds(order.index(rows[0]) * width, len(rows) * width)

    def react(rows, source, rates_ref, k):
        act, cols = split(side([HALF_LOG2E * jnp.log(1.0 + source[r] * source[r]) for r in rows])), columns(rows)
        for part in parts:
            exponent = jnp.dot(ord2[part, :], act, preferred_element_type=F32)
            rates = jnp.exp2(exponent + side([log_k[part, :]] * len(rows)))
            rates_ref[part, cols] = rates
            keep(rates_b, part, cols, rates)
        produced = gather(sto, rates_b, cols)
        for i, r in enumerate(rows):
            value = source[r] + TIME_STEP * produced[:, i * width:(i + 1) * width]
            field[k, r] = jnp.where(there, value, 0.0) if r == halo else value

    def react_back(rows, cells, rates_ref, put):
        cols = columns(rows)
        push = split(side([spread[r] for r in rows]))
        for part in parts:
            pulled = jnp.dot(sto2[part, :], push, preferred_element_type=F32)
            keep(grad_b, part, cols, rates_ref[part, cols] * pulled)
        summed = gather(ord_t, grad_b, cols)
        for i, r in enumerate(rows):
            c = cells[r]
            put(r, spread[r] + TIME_STEP * c / (1.0 + c * c) * summed[:, i * width:(i + 1) * width])

    def mix(p, k, r, back):
        ahead = admit[r] * smooth(k, r)
        mixed[p, 0, r] = jnp.where(rising[r], ahead, back[r])
        mixed[p, 1, r] = jnp.where(rising[r], back[r], ahead)

    def put_lam(r, value):
        lam[r] = value

    def put_out(r, value):
        out_adj[place(r)] = value

    last = depth - 1
    inner = [r for r in range(1, last)]

    react(late, conc, rates0, STAR0)
    pl.semaphore_wait(barrier, sum(1 if c is None else jnp.where(c, 1, 0) for c, _ in partners))
    edge_send(4)
    edge_send(5)
    for rows in early:
        react(rows, conc, rates0, STAR0)
    edge_send(STAR0)
    for copy in loads_cot:
        copy.wait()
    for r in reversed(inner):
        mix(0, STAR0, r, cot)
        send_raw(0, r)
    edge_wait(STAR0)
    if last:
        mix(0, STAR0, last, cot)
        send_raw(0, last)
    edge_wait(4)
    mix(0, STAR0, 0, cot)
    send_raw(0, 0)
    send_aslant(0)
    edge_wait(5)
    retain.append(aux_in[0:1] / (1.0 + aux_in[0:1]))
    admit.append(1.0 / (1.0 + aux_in[0:1]))
    rising.append(jnp.broadcast_to(aux_in[1:2], (species, width)) > 0.5)
    for r in [*reversed(inner), *([last] if last else []), 0, halo]:
        relay(0, r)

    def gain(r):
        ahead, back = collect(0, r)
        state[r] = ahead
        field[CARRY1, r] = admit[r] * back

    for rows in early:
        for r in rows:
            gain(r)
        if last in rows:
            edge_send(CARRY1)
        react(rows, state, rates1, STAR1)
    if last > 1:
        edge_send(STAR1)
    if depth > 1:
        gain(1)
        if last == 1:
            edge_send(CARRY1)
        react([1], state, rates1, STAR1)
        if last == 1:
            edge_send(STAR1)
    for rows in early:
        for r in rows:
            if r == last:
                edge_wait(CARRY1)
            spread[r] = smooth(CARRY1, r)
        react_back(rows, state, rates1, put_lam)
    for rows in early:
        for r in rows:
            if r == last:
                edge_wait(STAR1)
            mix(1, STAR1, r, lam)
            send_raw(1, r)
    gain(0)
    gain(halo)
    if last == 0:
        edge_send(CARRY1)
    react([0, halo], state, rates1, STAR1)
    if last == 0:
        edge_send(STAR1)
    for r in late:
        if r == last:
            edge_wait(CARRY1)
        spread[r] = smooth(CARRY1, r)
    react_back(late, state, rates1, put_lam)
    for r in late:
        if r == last:
            edge_wait(STAR1)
        mix(1, STAR1, r, lam)
        send_raw(1, r)
    send_aslant(1)
    for r in order:
        relay(1, r)

    def finish(r):
        ahead, back = collect(1, r)
        if r != halo:
            out_fin[place(r)] = ahead
        field[CARRY0, r] = admit[r] * back
        if r == last:
            edge_send(CARRY0)

    for rows in early:
        for r in rows:
            finish(r)
    for r in late:
        if r:
            finish(r)
    for rows in early:
        for r in rows:
            if r == last:
                edge_wait(CARRY0)
            spread[r] = smooth(CARRY0, r)
        react_back(rows, conc, rates0, put_out)
    finish(0)
    finish(halo)
    for r in late:
        if r == last:
            edge_wait(CARRY0)
        spread[r] = smooth(CARRY0, r)
    react_back(late, conc, rates0, put_out)

    for condition, make in drains:
        when(condition, lambda: make().wait_send())


def solution(mesh):
    sizes = (mesh.shape["gx"], mesh.shape["gy"], mesh.shape["row"])
    assert sizes[2] == 2

    def shards(conc, cotangent, courant, direction, rate_const, orders, stoich):
        species, slabs, depth, width = conc.shape
        reactions = orders.shape[0]
        assert slabs == 1
        direct = DIRECT if sizes[0] <= 4 else RELAY
        kinds = [direct] + [RELAY] * (depth - 1) + [direct]
        span = max(max([0, *raw, *led]) for raw, led in (plan(kind, sizes[0]) for kind in kinds)) or 1
        block = (depth, species, width)
        more = (depth + 1, species, width)
        one = (species, width)
        hbm = pl.BlockSpec(memory_space=pltpu.HBM)
        vmem = pl.BlockSpec(memory_space=pltpu.VMEM)
        cells = depth * width
        dma = pltpu.SemaphoreType.DMA
        outs = pl.pallas_call(
            functools.partial(kernel, sizes, kinds),
            name="flame_adjoint",
            out_shape=[jax.ShapeDtypeStruct(block, F32)] * 2,
            in_specs=[hbm] * 7,
            out_specs=[vmem, vmem],
            scratch_shapes=[
                pltpu.VMEM(block, F32), pltpu.VMEM(block, F32), pltpu.VMEM(more, F32), pltpu.VMEM(block, F32), pltpu.VMEM(block, F32),
                pltpu.VMEM((4,) + more, F32), pltpu.VMEM((4,) + one, F32),
                pltpu.VMEM((2, 2) + block, F32), pltpu.VMEM((2, 2) + one, F32), pltpu.VMEM((2, 2) + more, F32),
                pltpu.VMEM((2, 2, depth + 1, span) + one, F32),
                pltpu.VMEM((8, width), F32), pltpu.VMEM((8, width), F32),
                pltpu.VMEM((depth, width), F32), pltpu.VMEM((depth, width), jnp.int32), pltpu.VMEM((1, reactions), F32),
                pltpu.VMEM((reactions, cells), F32), pltpu.VMEM((reactions, cells + width), F32),
                pltpu.VMEM((2, reactions, cells + width), BF16), pltpu.VMEM((2, reactions, cells), BF16),
                pltpu.VMEM((species, reactions), jnp.int32), pltpu.VMEM((species, reactions), jnp.int32),
                pltpu.VMEM((reactions, 2 * species), BF16), pltpu.VMEM((species, reactions), BF16),
                pltpu.VMEM((reactions, 2 * species), BF16), pltpu.VMEM((species, reactions), BF16),
                pltpu.VMEM((reactions, width), F32),
                dma((2, depth)), dma((5,)),
                dma((2, 2, depth, span)), dma((2, 2, span + 1)), dma((2, 2, depth + 1, span)),
                dma((2, 2, depth + 1, span)), dma((2, 2)), dma((6,)), dma((6,)),
            ],
            compiler_params=pltpu.CompilerParams(collective_id=0, has_side_effects=True, vmem_limit_bytes=48 * 1024 * 1024),
        )(*[pltpu.with_memory_space_constraint(a, pltpu.HBM) for a in (conc, cotangent, courant, direction, rate_const.reshape(1, reactions), orders.T, stoich)])
        return tuple(out.transpose(1, 0, 2)[:, None] for out in outs)

    placed = (
        P(None, ("grp", "gx"), ("gy", "row"), None),
        P(None, ("grp", "gx"), ("gy", "row"), None),
        P(("grp", "gy", "row"), None),
        P(("grp", "gy", "row"), None),
        P(),
        P(),
        P(),
    )
    return jax.shard_map(
        shards,
        mesh=mesh,
        in_specs=placed,
        out_specs=(P(None, ("grp", "gx"), ("gy", "row"), None),) * 2,
        check_vma=False,
    )
```

```python
import functools

import jax
import jax.numpy as jnp
from jax import lax
from jax.experimental import pallas as pl
from jax.experimental.pallas import tpu as pltpu
from jax.sharding import PartitionSpec as P

MESH = pl.DeviceIdType.MESH
F32 = jnp.float32
BF16 = jnp.bfloat16
TIME_STEP = 0.1
DIFFUSION = 0.1
HALF_LOG2E = 0.5 * 1.4426950408889634
STAR0, CARRY1, STAR1, CARRY0 = range(4)
DIRECT, RELAY, PAIR, CHAIN = (0, 1, 2, 3), (0, 1, 2, 0), (0, 1, 0, 1), (0, 1, 0, 0)


def plan(kind, nx):
    raw, led = {}, {}
    for q in range(1, nx):
        count = kind[q] if q < len(kind) else 0
        for k in range(1, count + 1):
            raw.setdefault(k, []).append(q)
        if count < q:
            led.setdefault(count + 1, []).append(q)
    return raw, led


def member(q, places):
    found, places = None, sorted(places)
    while places:
        size = 1
        while size < len(places) and places[size] == places[0] + size:
            size += 1
        run = (q >= places[0]) & (q <= places[size - 1])
        found = run if found is None else found | run
        places = places[size:]
    return found


def kernel(
    sizes, kinds, relays, conc_hbm, cot_hbm, cour_hbm, dir_hbm, const_hbm, ord_hbm, sto_hbm, out_fin, out_adj,
    conc, cot, state, spread, lam, field, sib, mixed, mixed_h, swept, recv, aux_out, aux_in,
    cour_v, dir_v, const_v, rates0, rates1, rates_b, grad_b,
    ord_i, sto_i, ord2, ord_t, sto2, sto, log_k,
    in_sem, tab_sem, send_sem, dsend_sem, recv_sem, lsend_sem, wrecv_sem, esend_sem, erecv_sem,
):
    nx, ngy, nrow = sizes
    depth, species, width = conc.shape
    halo = depth
    reactions = ord_i.shape[1]
    late = [1, 0] if depth > 1 else [0]
    early = [list(range(r, min(r + 2, depth))) for r in range(2, depth, 2)]
    order = [r for rows in early for r in rows] + late + [halo]
    chunk = min(256, reactions)
    plans = [[plan(kind, nx) for kind in row_kinds] for row_kinds in kinds]
    spans = [[max([0, *raw, *led]) for raw, led in row_plans] for row_plans in plans]

    x = lax.axis_index("gx")
    gy = lax.axis_index("gy")
    row = lax.axis_index("row")
    q_of = [x, nx - 1 - x]
    there = jnp.where(row == 0, gy > 0, gy < ngy - 1)
    across = {"gy": gy + 2 * row - 1, "row": 1 - row}
    beside = {"row": 1 - row}

    def place(r):
        return r + row * (depth - 1 - 2 * r)

    def load(source, target, base):
        return [pltpu.make_async_copy(source.at[:, 0, r, :], target.at[place(r)], in_sem.at[base, r]) for r in range(depth)]

    loads_conc = load(conc_hbm, conc, 0)
    loads_cot = load(cot_hbm, cot, 1)
    tables = [pltpu.make_async_copy(a, b, tab_sem.at[i]) for i, (a, b) in enumerate(
        ((ord_hbm, ord_i), (sto_hbm, sto_i), (const_hbm, const_v), (cour_hbm, cour_v), (dir_hbm, dir_v)))]
    for copy in tables + loads_conc + loads_cot:
        copy.start()

    def inside(target):
        return (target >= 0) & (target < nx)

    own_span, halo_span = max(max(row_spans[:depth]) for row_spans in spans), max(row_spans[halo] for row_spans in spans)
    partners = [(None, beside)]
    for k in range(1, max(own_span, halo_span) + 1):
        for sign in (1, -1):
            partners.append((inside(x + sign * k), {"gx": x + sign * k}))
    partners.append((there, across))
    for k in range(1, halo_span + 1):
        for sign in (1, -1):
            partners.append((there & inside(x + sign * k), {"gx": x + sign * k, **across}))

    def when(condition, action):
        if condition is None:
            action()
        else:
            pl.when(condition)(action)

    barrier = pltpu.get_barrier_semaphore()
    for condition, device in partners:
        when(condition, lambda: pl.semaphore_signal(barrier, inc=1, device_id=device, device_id_type=MESH))

    def nothing(ref, *index):
        ref[index] = jnp.zeros_like(ref[index])

    for d in range(2):
        missing = {}
        for p in range(2):
            for r in range(depth + 1):
                raw, led = plans[p][r]
                for k in range(1, spans[p][r] + 1):
                    missing.setdefault((r == halo, *sorted(raw.get(k, []) + led.get(k, []))), []).append((p, d, r, k - 1))
        for (outer, *places), slots in missing.items():
            got = member(q_of[d], places)

            @pl.when(jnp.logical_not(got & there if outer else got))
            def _():
                for slot in slots:
                    nothing(recv, *slot)

    @pl.when(jnp.logical_not(there))
    def _():
        nothing(field, STAR0, halo)
        nothing(aux_in, slice(None))
        for p in range(2):
            for d in range(2):
                nothing(mixed_h, p, d)

    for copy in tables:
        copy.wait()

    def pick(ref, r):
        return jnp.where(row == 0, ref[r:r + 1], ref[depth - 1 - r:depth - r])

    courant = [pick(cour_v, r) for r in range(depth)]
    upward = [pick(dir_v, r).astype(F32) for r in range(depth)]
    aux_out[...] = jnp.zeros_like(aux_out)
    aux_out[0:1] = courant[0]
    aux_out[1:2] = upward[0]
    retain = [c / (1.0 + c) for c in courant]
    admit = [1.0 / (1.0 + c) for c in courant]
    rising = [jnp.broadcast_to(u, (species, width)) > 0.5 for u in upward]

    order_float = ord_i[...].astype(F32)
    order_trans = order_float.T.astype(BF16)
    ord2[:, :species] = order_trans
    ord2[:, species:] = order_trans
    stoich_float = sto_i[...].astype(F32)
    sto[...] = stoich_float.astype(BF16)
    log_k[...] = jnp.broadcast_to(jnp.log(const_v[...]) * (2.0 * HALF_LOG2E), (width, reactions)).T
    for copy in loads_conc:
        copy.wait()

    drains = []

    def begin(condition, make):
        when(condition, lambda: make().start())
        drains.append((condition, make))

    def along(p, d, r, k, source, swept_value):
        return pltpu.make_async_remote_copy(
            src_ref=source, dst_ref=recv.at[p, d, r, k - 1],
            send_sem=(lsend_sem if swept_value else send_sem).at[p, d, r, k - 1], recv_sem=recv_sem.at[p, d, r, k - 1],
            device_id={"gx": x + k * (1 - 2 * d)}, device_id_type=MESH)

    def aslant(p, d, k):
        return pltpu.make_async_remote_copy(
            src_ref=mixed.at[p, d, 0], dst_ref=mixed_h.at[p, d] if k == 0 else recv.at[p, d, halo, k - 1],
            send_sem=dsend_sem.at[p, d, k], recv_sem=wrecv_sem.at[p, d] if k == 0 else recv_sem.at[p, d, halo, k - 1],
            device_id={"gx": x + k * (1 - 2 * d), **across} if k else across, device_id_type=MESH)

    def send_raw(p, r):
        for k in sorted(plans[p][r][0], reverse=True):
            for d in range(2):
                begin(member(q_of[d], [q - k for q in plans[p][r][0][k]]), functools.partial(along, p, d, r, k, mixed.at[p, d, r], False))

    def send_aslant(p):
        for k in sorted(plans[p][halo][0], reverse=True):
            for d in range(2):
                begin(there & member(q_of[d], [q - k for q in plans[p][halo][0][k]]), functools.partial(aslant, p, d, k))
        for d in range(2):
            begin(there, functools.partial(aslant, p, d, 0))

    def arrivals(p, d, r):
        raw, led = plans[p][r]
        if r == halo:
            yield there, aslant(p, d, 0)
        for k in range(1, spans[p][r] + 1):
            for table in (raw, led):
                if k in table:
                    got = member(q_of[d], table[k])
                    yield got & there if r == halo and table is raw else got, along(p, d, r, k, recv.at[p, d, r, k - 1], False)

    def passing(p, r, places=None):
        return [q - k for k, got in plans[p][r][1].items() for q in got if places is None or q - k in places]

    def total(p, d, r):
        value = mixed_h[p, d] if r == halo else mixed[p, d, r]
        carried = None
        for k in range(spans[p][r], 0, -1):
            carried = recv[p, d, r, k - 1] if carried is None else recv[p, d, r, k - 1] + retain[r] * carried
        return value if carried is None else value + retain[r] * carried

    def relay(p, r, places):
        for d in range(2):
            if not passing(p, r, places):
                continue

            @pl.when(member(q_of[d], passing(p, r, places)))
            def _():
                for got, copy in arrivals(p, d, r):
                    pl.when(got)(copy.wait_recv)
                swept[p, d, r] = total(p, d, r)
            for k, got in plans[p][r][1].items():
                senders = [q - k for q in got if q - k in places]
                if senders:
                    begin(member(q_of[d], senders), functools.partial(along, p, d, r, k, swept.at[p, d, r], True))

    def collect(p, r):
        for d in range(2):
            for got, copy in arrivals(p, d, r):
                if passing(p, r):
                    got = got & jnp.logical_not(member(q_of[d], passing(p, r)))
                pl.when(got)(copy.wait_recv)
        ahead, back = total(p, 0, r), total(p, 1, r)
        return jnp.where(rising[r], ahead, back), jnp.where(rising[r], back, ahead)

    def edge_copy(k):
        if k < 4:
            return pltpu.make_async_remote_copy(
                src_ref=field.at[k, depth - 1], dst_ref=sib.at[k], send_sem=esend_sem.at[k], recv_sem=erecv_sem.at[k],
                device_id=beside, device_id_type=MESH)
        source, target = ((field.at[STAR0, 0], field.at[STAR0, halo]), (aux_out, aux_in))[k - 4]
        return pltpu.make_async_remote_copy(
            src_ref=source, dst_ref=target, send_sem=esend_sem.at[k], recv_sem=erecv_sem.at[k],
            device_id=across, device_id_type=MESH)

    def edge_send(k):
        begin(None if k < 4 else there, functools.partial(edge_copy, k))

    def edge_wait(k):
        when(None if k < 4 else there, lambda: edge_copy(k).wait_recv())

    lane = lax.broadcasted_iota(jnp.int32, (species, width), 1)

    def smooth(k, r):
        here = field[k, r]
        below = field[k, halo] if r == 0 else field[k, r - 1]
        above = sib[k] if r == depth - 1 else field[k, r + 1]
        before = jnp.where(lane == 0, 0.0, pltpu.roll(here, 1, 1))
        after = jnp.where(lane == width - 1, 0.0, pltpu.roll(here, width - 1, 1))
        return here + DIFFUSION * (above + below + after + before - 4.0 * here)

    def side(parts):
        return parts[0] if len(parts) == 1 else jnp.concatenate(parts, axis=1)

    def split(value):
        high = value.astype(BF16)
        low = (value - high.astype(F32)).astype(BF16)
        return jnp.concatenate([high, low], axis=0)

    parts = [pl.ds(i, chunk) for i in range(0, reactions, chunk)]

    def keep(target, part, cols, value):
        high = value.astype(BF16)
        target[0, part, cols] = high
        target[1, part, cols] = (value - high.astype(F32)).astype(BF16)

    def gather(table, halves, cols):
        small = jnp.dot(table[...], halves[1, :, cols], preferred_element_type=F32)
        return small + jnp.dot(table[...], halves[0, :, cols], preferred_element_type=F32)

    def columns(rows):
        return pl.ds(order.index(rows[0]) * width, len(rows) * width)

    def react(rows, source, rates_ref, k):
        act, cols = split(side([HALF_LOG2E * jnp.log(1.0 + source[r] * source[r]) for r in rows])), columns(rows)
        for part in parts:
            exponent = jnp.dot(ord2[part, :], act, preferred_element_type=F32)
            rates = jnp.exp2(exponent + side([log_k[part, :]] * len(rows)))
            rates_ref[part, cols] = rates
            keep(rates_b, part, cols, rates)
        produced = gather(sto, rates_b, cols)
        for i, r in enumerate(rows):
            value = source[r] + TIME_STEP * produced[:, i * width:(i + 1) * width]
            field[k, r] = jnp.where(there, value, 0.0) if r == halo else value

    def react_back(rows, cells, rates_ref, put):
        cols = columns(rows)
        push = split(side([spread[r] for r in rows]))
        for part in parts:
            pulled = jnp.dot(sto2[part, :], push, preferred_element_type=F32)
            keep(grad_b, part, cols, rates_ref[part, cols] * pulled)
        summed = gather(ord_t, grad_b, cols)
        for i, r in enumerate(rows):
            c = cells[r]
            put(r, spread[r] + TIME_STEP * c / (1.0 + c * c) * summed[:, i * width:(i + 1) * width])

    def mix(p, k, r, back):
        ahead = admit[r] * smooth(k, r)
        mixed[p, 0, r] = jnp.where(rising[r], ahead, back[r])
        mixed[p, 1, r] = jnp.where(rising[r], back[r], ahead)

    def put_lam(r, value):
        lam[r] = value

    def put_out(r, value):
        out_adj[place(r)] = value

    last = depth - 1
    inner = [r for r in range(1, last)]

    react(late, conc, rates0, STAR0)
    pl.semaphore_wait(barrier, sum(1 if c is None else jnp.where(c, 1, 0) for c, _ in partners))
    edge_send(4)
    edge_send(5)
    for rows in early:
        react(rows, conc, rates0, STAR0)
    edge_send(STAR0)
    ord_t[...] = ord_i[...].astype(F32).astype(BF16)
    stoich_trans = sto_i[...].astype(F32).T.astype(BF16)
    sto2[:, :species] = stoich_trans
    sto2[:, species:] = stoich_trans
    for copy in loads_cot:
        copy.wait()
    for r in reversed(inner):
        mix(0, STAR0, r, cot)
        send_raw(0, r)
    edge_wait(STAR0)
    if last:
        mix(0, STAR0, last, cot)
        send_raw(0, last)
    edge_wait(4)
    mix(0, STAR0, 0, cot)
    send_raw(0, 0)
    send_aslant(0)
    edge_wait(5)
    retain.append(aux_in[0:1] / (1.0 + aux_in[0:1]))
    admit.append(1.0 / (1.0 + aux_in[0:1]))
    rising.append(jnp.broadcast_to(aux_in[1:2], (species, width)) > 0.5)
    for r, places in relays[0]:
        relay(0, r, places)

    def gain(r):
        ahead, back = collect(0, r)
        state[r] = ahead
        field[CARRY1, r] = admit[r] * back

    for rows in early:
        for r in rows:
            gain(r)
        if last in rows:
            edge_send(CARRY1)
        react(rows, state, rates1, STAR1)
    if last > 1:
        edge_send(STAR1)
    if depth > 1:
        gain(1)
        if last == 1:
            edge_send(CARRY1)
        react([1], state, rates1, STAR1)
        if last == 1:
            edge_send(STAR1)
    for rows in early:
        for r in rows:
            if r == last:
                edge_wait(CARRY1)
            spread[r] = smooth(CARRY1, r)
        react_back(rows, state, rates1, put_lam)
    for rows in early:
        for r in rows:
            if r == last:
                edge_wait(STAR1)
            mix(1, STAR1, r, lam)
            send_raw(1, r)
    gain(0)
    gain(halo)
    if last == 0:
        edge_send(CARRY1)
    react([0, halo], state, rates1, STAR1)
    if last == 0:
        edge_send(STAR1)
    for r in late:
        if r == last:
            edge_wait(CARRY1)
        spread[r] = smooth(CARRY1, r)
    react_back(late, state, rates1, put_lam)
    for r in late:
        if r == last:
            edge_wait(STAR1)
        mix(1, STAR1, r, lam)
        send_raw(1, r)
    send_aslant(1)
    for r, places in relays[1]:
        relay(1, r, places)

    def finish(r):
        ahead, back = collect(1, r)
        if r != halo:
            out_fin[place(r)] = ahead
        field[CARRY0, r] = admit[r] * back
        if r == last:
            edge_send(CARRY0)

    for rows in early:
        for r in rows:
            finish(r)
    for r in late:
        if r:
            finish(r)
    for rows in early:
        for r in rows:
            if r == last:
                edge_wait(CARRY0)
            spread[r] = smooth(CARRY0, r)
        react_back(rows, conc, rates0, put_out)
    finish(0)
    finish(halo)
    for r in late:
        if r == last:
            edge_wait(CARRY0)
        spread[r] = smooth(CARRY0, r)
    react_back(late, conc, rates0, put_out)

    for condition, make in drains:
        when(condition, lambda: make().wait_send())


def solution(mesh):
    sizes = (mesh.shape["gx"], mesh.shape["gy"], mesh.shape["row"])
    assert sizes[2] == 2

    def shards(conc, cotangent, courant, direction, rate_const, orders, stoich):
        species, slabs, depth, width = conc.shape
        reactions = orders.shape[0]
        assert slabs == 1
        kinds, relays = [[CHAIN] * (depth + 1)] * 2, [[(r, range(sizes[0])) for r in range(depth + 1)]] * 2
        if sizes[0] <= 4 and depth == 4:
            kinds, relays = [[PAIR,PAIR,PAIR,RELAY,RELAY],[PAIR,RELAY,PAIR,PAIR,PAIR]], [[(r, [q]) for r, q in steps] for steps in [[(2, 1), (1, 1), (3, 2), (0, 1), (4, 2)], [(2, 1), (3, 1), (1, 2), (0, 1), (4, 1)]]]
        span = max(max([0, *raw, *led]) for row_kinds in kinds for raw, led in (plan(kind, sizes[0]) for kind in row_kinds)) or 1
        block = (depth, species, width)
        more = (depth + 1, species, width)
        one = (species, width)
        hbm = pl.BlockSpec(memory_space=pltpu.HBM)
        vmem = pl.BlockSpec(memory_space=pltpu.VMEM)
        cells = depth * width
        dma = pltpu.SemaphoreType.DMA
        outs = pl.pallas_call(
            functools.partial(kernel, sizes, kinds, relays),
            name="flame_adjoint",
            out_shape=[jax.ShapeDtypeStruct(block, F32)] * 2,
            in_specs=[hbm] * 7,
            out_specs=[vmem, vmem],
            scratch_shapes=[
                pltpu.VMEM(block, F32), pltpu.VMEM(block, F32), pltpu.VMEM(more, F32), pltpu.VMEM(block, F32), pltpu.VMEM(block, F32),
                pltpu.VMEM((4,) + more, F32), pltpu.VMEM((4,) + one, F32),
                pltpu.VMEM((2, 2) + block, F32), pltpu.VMEM((2, 2) + one, F32), pltpu.VMEM((2, 2) + more, F32),
                pltpu.VMEM((2, 2, depth + 1, span) + one, F32),
                pltpu.VMEM((8, width), F32), pltpu.VMEM((8, width), F32),
                pltpu.VMEM((depth, width), F32), pltpu.VMEM((depth, width), jnp.int32), pltpu.VMEM((1, reactions), F32),
                pltpu.VMEM((reactions, cells), F32), pltpu.VMEM((reactions, cells + width), F32),
                pltpu.VMEM((2, reactions, cells + width), BF16), pltpu.VMEM((2, reactions, cells), BF16),
                pltpu.VMEM((species, reactions), jnp.int32), pltpu.VMEM((species, reactions), jnp.int32),
                pltpu.VMEM((reactions, 2 * species), BF16), pltpu.VMEM((species, reactions), BF16),
                pltpu.VMEM((reactions, 2 * species), BF16), pltpu.VMEM((species, reactions), BF16),
                pltpu.VMEM((reactions, width), F32),
                dma((2, depth)), dma((5,)),
                dma((2, 2, depth, span)), dma((2, 2, span + 1)), dma((2, 2, depth + 1, span)),
                dma((2, 2, depth + 1, span)), dma((2, 2)), dma((6,)), dma((6,)),
            ],
            compiler_params=pltpu.CompilerParams(collective_id=0, has_side_effects=True, vmem_limit_bytes=48 * 1024 * 1024),
        )(*[pltpu.with_memory_space_constraint(a, pltpu.HBM) for a in (conc, cotangent, courant, direction, rate_const.reshape(1, reactions), orders.T, stoich)])
        return tuple(out.transpose(1, 0, 2)[:, None] for out in outs)

    placed = (
        P(None, ("grp", "gx"), ("gy", "row"), None),
        P(None, ("grp", "gx"), ("gy", "row"), None),
        P(("grp", "gy", "row"), None),
        P(("grp", "gy", "row"), None),
        P(),
        P(),
        P(),
    )
    return jax.shard_map(
        shards,
        mesh=mesh,
        in_specs=placed,
        out_specs=(P(None, ("grp", "gx"), ("gy", "row"), None),) * 2,
        check_vma=False,
    )
```

```python
import functools

import jax
import jax.numpy as jnp
from jax import lax
from jax.experimental import pallas as pl
from jax.experimental.pallas import tpu as pltpu
from jax.sharding import PartitionSpec as P

MESH = pl.DeviceIdType.MESH
F32 = jnp.float32
BF16 = jnp.bfloat16
TIME_STEP = 0.1
DIFFUSION = 0.1
HALF_LOG2E = 0.5 * 1.4426950408889634
STAR0, CARRY1, STAR1, CARRY0 = range(4)
DIRECT, RELAY, PAIR, CHAIN = (0, 1, 2, 3), (0, 1, 2, 0), (0, 1, 0, 1), (0, 1, 0, 0)


def plan(kind, nx):
    raw, led = {}, {}
    for q in range(1, nx):
        count = kind[q] if q < len(kind) else 0
        for k in range(1, count + 1):
            raw.setdefault(k, []).append(q)
        if count < q:
            led.setdefault(count + 1, []).append(q)
    return raw, led


def member(q, places):
    found, places = None, sorted(places)
    while places:
        size = 1
        while size < len(places) and places[size] == places[0] + size:
            size += 1
        run = (q >= places[0]) & (q <= places[size - 1])
        found = run if found is None else found | run
        places = places[size:]
    return found


def kernel(
    sizes, kinds, relays, conc_hbm, cot_hbm, cour_hbm, dir_hbm, const_hbm, ord_hbm, sto_hbm, out,
    conc, cot, state, spread, lam, field, sib, mixed, mixed_h, swept, recv, aux_out, aux_in,
    cour_v, dir_v, const_v, rates0, rates1, rates_b, grad_b,
    ord_i, sto_i, ord2, ord_t, sto2, sto, log_k,
    in_sem, tab_sem, send_sem, dsend_sem, recv_sem, lsend_sem, wrecv_sem, esend_sem, erecv_sem,
):
    nx, ngy, nrow = sizes
    depth, species, width = conc.shape
    halo = depth
    reactions = ord_i.shape[1]
    late = [1, 0] if depth > 1 else [0]
    early = [list(range(r, min(r + 2, depth))) for r in range(2, depth, 2)]
    ends = sorted({0, depth - 1})
    inner = list(range(1, depth - 1))
    order = [r for rows in early for r in rows] + late + [halo]
    spots = {STAR0: ends + inner, STAR1: order}
    chunk = min(256, reactions)
    plans = [[plan(kind, nx) for kind in row_kinds] for row_kinds in kinds]
    spans = [[max([0, *raw, *led]) for raw, led in row_plans] for row_plans in plans]

    x = lax.axis_index("gx")
    gy = lax.axis_index("gy")
    row = lax.axis_index("row")
    q_of = [x, nx - 1 - x]
    there = jnp.where(row == 0, gy > 0, gy < ngy - 1)
    across = {"gy": gy + 2 * row - 1, "row": 1 - row}
    beside = {"row": 1 - row}

    def place(r):
        return r + row * (depth - 1 - 2 * r)

    def load(source, target, base):
        return [pltpu.make_async_copy(source.at[:, 0, r, :], target.at[place(r)], in_sem.at[base, r]) for r in range(depth)]

    loads_conc = load(conc_hbm, conc, 0)
    loads_cot = load(cot_hbm, cot, 1)
    tables = [pltpu.make_async_copy(a, b, tab_sem.at[i]) for i, (a, b) in enumerate(
        ((ord_hbm, ord_i), (sto_hbm, sto_i), (const_hbm, const_v), (cour_hbm, cour_v), (dir_hbm, dir_v)))]
    for copy in tables + loads_conc + loads_cot:
        copy.start()

    def inside(target):
        return (target >= 0) & (target < nx)

    own_span, halo_span = max(max(row_spans[:depth]) for row_spans in spans), max(row_spans[halo] for row_spans in spans)
    partners = [(None, beside)]
    for k in range(1, max(own_span, halo_span) + 1):
        for sign in (1, -1):
            partners.append((inside(x + sign * k), {"gx": x + sign * k}))
    partners.append((there, across))
    for k in range(1, halo_span + 1):
        for sign in (1, -1):
            partners.append((there & inside(x + sign * k), {"gx": x + sign * k, **across}))

    def when(condition, action):
        if condition is None:
            action()
        else:
            pl.when(condition)(action)

    barrier = pltpu.get_barrier_semaphore()
    for condition, device in partners:
        when(condition, lambda: pl.semaphore_signal(barrier, inc=1, device_id=device, device_id_type=MESH))

    def nothing(ref, *index):
        ref[index] = jnp.zeros_like(ref[index])

    for d in range(2):
        missing = {}
        for p in range(2):
            for r in range(depth + 1):
                raw, led = plans[p][r]
                for k in range(1, spans[p][r] + 1):
                    missing.setdefault((r == halo, *sorted(raw.get(k, []) + led.get(k, []))), []).append((p, d, r, k - 1))
        for (outer, *places), slots in missing.items():
            got = member(q_of[d], places)

            @pl.when(jnp.logical_not(got & there if outer else got))
            def _():
                for slot in slots:
                    nothing(recv, *slot)

    @pl.when(jnp.logical_not(there))
    def _():
        nothing(field, STAR0, halo)
        nothing(aux_in, slice(None))
        for p in range(2):
            for d in range(2):
                nothing(mixed_h, p, d)

    for copy in tables:
        copy.wait()

    def pick(ref, r):
        return jnp.where(row == 0, ref[r:r + 1], ref[depth - 1 - r:depth - r])

    courant = [pick(cour_v, r) for r in range(depth)]
    upward = [pick(dir_v, r).astype(F32) for r in range(depth)]
    aux_out[...] = jnp.zeros_like(aux_out)
    aux_out[0:1] = courant[0]
    aux_out[1:2] = upward[0]
    retain = [c / (1.0 + c) for c in courant]
    admit = [1.0 / (1.0 + c) for c in courant]
    rising = [jnp.broadcast_to(u, (species, width)) > 0.5 for u in upward]

    order_float = ord_i[...].astype(F32)
    order_trans = order_float.T.astype(BF16)
    ord2[:, :species] = order_trans
    ord2[:, species:] = order_trans
    stoich_float = sto_i[...].astype(F32)
    sto[...] = stoich_float.astype(BF16)
    log_k[...] = jnp.broadcast_to(jnp.log(const_v[...]) * (2.0 * HALF_LOG2E), (width, reactions)).T
    for copy in loads_conc:
        copy.wait()

    drains = []

    def begin(condition, make):
        when(condition, lambda: make().start())
        drains.append((condition, make))

    def along(p, d, r, k, source, swept_value):
        return pltpu.make_async_remote_copy(
            src_ref=source, dst_ref=recv.at[p, d, r, k - 1],
            send_sem=(lsend_sem if swept_value else send_sem).at[p, d, r, k - 1], recv_sem=recv_sem.at[p, d, r, k - 1],
            device_id={"gx": x + k * (1 - 2 * d)}, device_id_type=MESH)

    def aslant(p, d, k):
        return pltpu.make_async_remote_copy(
            src_ref=mixed.at[p, d, 0], dst_ref=mixed_h.at[p, d] if k == 0 else recv.at[p, d, halo, k - 1],
            send_sem=dsend_sem.at[p, d, k], recv_sem=wrecv_sem.at[p, d] if k == 0 else recv_sem.at[p, d, halo, k - 1],
            device_id={"gx": x + k * (1 - 2 * d), **across} if k else across, device_id_type=MESH)

    def send_raw(p, r):
        for k in sorted(plans[p][r][0], reverse=True):
            for d in range(2):
                begin(member(q_of[d], [q - k for q in plans[p][r][0][k]]), functools.partial(along, p, d, r, k, mixed.at[p, d, r], False))

    def send_aslant(p):
        for k in sorted(plans[p][halo][0], reverse=True):
            for d in range(2):
                begin(there & member(q_of[d], [q - k for q in plans[p][halo][0][k]]), functools.partial(aslant, p, d, k))
        for d in range(2):
            begin(there, functools.partial(aslant, p, d, 0))

    def arrivals(p, d, r):
        raw, led = plans[p][r]
        if r == halo:
            yield there, aslant(p, d, 0)
        for k in range(1, spans[p][r] + 1):
            for table in (raw, led):
                if k in table:
                    got = member(q_of[d], table[k])
                    yield got & there if r == halo and table is raw else got, along(p, d, r, k, recv.at[p, d, r, k - 1], False)

    def passing(p, r, places=None):
        return [q - k for k, got in plans[p][r][1].items() for q in got if places is None or q - k in places]

    def total(p, d, r):
        value = mixed_h[p, d] if r == halo else mixed[p, d, r]
        carried = None
        for k in range(spans[p][r], 0, -1):
            carried = recv[p, d, r, k - 1] if carried is None else recv[p, d, r, k - 1] + retain[r] * carried
        return value if carried is None else value + retain[r] * carried

    def relay(p, r, places):
        for d in range(2):
            if not passing(p, r, places):
                continue

            @pl.when(member(q_of[d], passing(p, r, places)))
            def _():
                for got, copy in arrivals(p, d, r):
                    pl.when(got)(copy.wait_recv)
                swept[p, d, r] = total(p, d, r)
            for k, got in plans[p][r][1].items():
                senders = [q - k for q in got if q - k in places]
                if senders:
                    begin(member(q_of[d], senders), functools.partial(along, p, d, r, k, swept.at[p, d, r], True))

    def collect(p, r):
        for d in range(2):
            for got, copy in arrivals(p, d, r):
                if passing(p, r):
                    got = got & jnp.logical_not(member(q_of[d], passing(p, r)))
                pl.when(got)(copy.wait_recv)
        ahead, back = total(p, 0, r), total(p, 1, r)
        return jnp.where(rising[r], ahead, back), jnp.where(rising[r], back, ahead)

    def edge_copy(k):
        if k < 4:
            return pltpu.make_async_remote_copy(
                src_ref=field.at[k, depth - 1], dst_ref=sib.at[k], send_sem=esend_sem.at[k], recv_sem=erecv_sem.at[k],
                device_id=beside, device_id_type=MESH)
        source, target = ((field.at[STAR0, 0], field.at[STAR0, halo]), (aux_out, aux_in))[k - 4]
        return pltpu.make_async_remote_copy(
            src_ref=source, dst_ref=target, send_sem=esend_sem.at[k], recv_sem=erecv_sem.at[k],
            device_id=across, device_id_type=MESH)

    def edge_send(k):
        begin(None if k < 4 else there, functools.partial(edge_copy, k))

    def edge_wait(k):
        when(None if k < 4 else there, lambda: edge_copy(k).wait_recv())

    lane = lax.broadcasted_iota(jnp.int32, (species, width), 1)

    def smooth(k, r):
        here = field[k, r]
        below = field[k, halo] if r == 0 else field[k, r - 1]
        above = sib[k] if r == depth - 1 else field[k, r + 1]
        before = jnp.where(lane == 0, 0.0, pltpu.roll(here, 1, 1))
        after = jnp.where(lane == width - 1, 0.0, pltpu.roll(here, width - 1, 1))
        return here + DIFFUSION * (above + below + after + before - 4.0 * here)

    def side(parts):
        return parts[0] if len(parts) == 1 else jnp.concatenate(parts, axis=1)

    def split(value):
        high = value.astype(BF16)
        low = (value - high.astype(F32)).astype(BF16)
        return jnp.concatenate([high, low], axis=0)

    parts = [pl.ds(i, chunk) for i in range(0, reactions, chunk)]

    def keep(target, part, cols, value):
        high = value.astype(BF16)
        target[0, part, cols] = high
        target[1, part, cols] = (value - high.astype(F32)).astype(BF16)

    def gather(table, halves, cols):
        small = jnp.dot(table[...], halves[1, :, cols], preferred_element_type=F32)
        return small + jnp.dot(table[...], halves[0, :, cols], preferred_element_type=F32)

    def columns(listed, rows):
        return pl.ds(listed.index(rows[0]) * width, len(rows) * width)

    def react(rows, source, rates_ref, k):
        act, cols = split(side([HALF_LOG2E * jnp.log(1.0 + source[r] * source[r]) for r in rows])), columns(spots[k], rows)
        for part in parts:
            exponent = jnp.dot(ord2[part, :], act, preferred_element_type=F32)
            rates = jnp.exp2(exponent + side([log_k[part, :]] * len(rows)))
            rates_ref[part, cols] = rates
            keep(rates_b, part, cols, rates)
        produced = gather(sto, rates_b, cols)
        for i, r in enumerate(rows):
            value = source[r] + TIME_STEP * produced[:, i * width:(i + 1) * width]
            field[k, r] = jnp.where(there, value, 0.0) if r == halo else value

    def react_back(rows, cells, rates_ref, k, put):
        cols = columns(order, rows)
        push = split(side([spread[r] for r in rows]))
        for part in parts:
            pulled = jnp.dot(sto2[part, :], push, preferred_element_type=F32)
            keep(grad_b, part, cols, side([rates_ref[part, columns(spots[k], [r])] for r in rows]) * pulled)
        summed = gather(ord_t, grad_b, cols)
        for i, r in enumerate(rows):
            c = cells[r]
            put(r, spread[r] + TIME_STEP * c / (1.0 + c * c) * summed[:, i * width:(i + 1) * width])

    def mix(p, k, r, back):
        ahead = admit[r] * smooth(k, r)
        mixed[p, 0, r] = jnp.where(rising[r], ahead, back[r])
        mixed[p, 1, r] = jnp.where(rising[r], back[r], ahead)

    def put(target, r, value):
        for side_row in range(2):
            @pl.when(row == side_row)
            def _():
                out[target, :, 0, depth - 1 - r if side_row else r, :] = value

    def put_lam(r, value):
        lam[r] = value

    def put_out(r, value):
        put(1, r, value)

    last = depth - 1

    react(ends, conc, rates0, STAR0)
    pl.semaphore_wait(barrier, sum(1 if c is None else jnp.where(c, 1, 0) for c, _ in partners))
    edge_send(4)
    edge_send(STAR0)
    edge_send(5)
    for i in range(0, len(inner), 2):
        react(inner[i:i + 2], conc, rates0, STAR0)
    for copy in loads_cot:
        copy.wait()
    edge_wait(STAR0)
    for r in [*range(2, depth), 1][:last]:
        mix(0, STAR0, r, cot)
        send_raw(0, r)
    ord_t[...] = ord_i[...].astype(F32).astype(BF16)
    stoich_trans = sto_i[...].astype(F32).T.astype(BF16)
    sto2[:, :species] = stoich_trans
    sto2[:, species:] = stoich_trans
    edge_wait(4)
    mix(0, STAR0, 0, cot)
    send_aslant(0)
    send_raw(0, 0)
    edge_wait(5)
    retain.append(aux_in[0:1] / (1.0 + aux_in[0:1]))
    admit.append(1.0 / (1.0 + aux_in[0:1]))
    rising.append(jnp.broadcast_to(aux_in[1:2], (species, width)) > 0.5)
    for r, places in relays[0]:
        relay(0, r, places)

    def gain(r):
        ahead, back = collect(0, r)
        state[r] = ahead
        field[CARRY1, r] = admit[r] * back

    for rows in early:
        for r in rows:
            gain(r)
        if last in rows:
            edge_send(CARRY1)
        react(rows, state, rates1, STAR1)
    if last > 1:
        edge_send(STAR1)
    if depth > 1:
        gain(1)
        if last == 1:
            edge_send(CARRY1)
        react([1], state, rates1, STAR1)
        if last == 1:
            edge_send(STAR1)
    for rows in early:
        for r in rows:
            if r == last:
                edge_wait(CARRY1)
            spread[r] = smooth(CARRY1, r)
        react_back(rows, state, rates1, STAR1, put_lam)
    for rows in early:
        for r in rows:
            if r == last:
                edge_wait(STAR1)
            mix(1, STAR1, r, lam)
            send_raw(1, r)
    gain(0)
    gain(halo)
    if last == 0:
        edge_send(CARRY1)
    react([0, halo], state, rates1, STAR1)
    if last == 0:
        edge_send(STAR1)
    for r in late:
        if r == last:
            edge_wait(CARRY1)
        spread[r] = smooth(CARRY1, r)
    react_back(late, state, rates1, STAR1, put_lam)
    for r in late:
        if r == last:
            edge_wait(STAR1)
        mix(1, STAR1, r, lam)
        send_raw(1, r)
    send_aslant(1)
    for r, places in relays[1]:
        relay(1, r, places)

    def finish(r):
        ahead, back = collect(1, r)
        if r != halo:
            put(0, r, ahead)
        field[CARRY0, r] = admit[r] * back
        if r == last:
            edge_send(CARRY0)

    for rows in early:
        for r in rows:
            finish(r)
    for r in late:
        if r:
            finish(r)
    for rows in early:
        for r in rows:
            if r == last:
                edge_wait(CARRY0)
            spread[r] = smooth(CARRY0, r)
        react_back(rows, conc, rates0, STAR0, put_out)
    finish(0)
    finish(halo)
    for r in late:
        if r == last:
            edge_wait(CARRY0)
        spread[r] = smooth(CARRY0, r)
    react_back(late, conc, rates0, STAR0, put_out)

    for condition, make in drains:
        when(condition, lambda: make().wait_send())


def solution(mesh):
    sizes = (mesh.shape["gx"], mesh.shape["gy"], mesh.shape["row"])
    assert sizes[2] == 2

    def shards(conc, cotangent, courant, direction, rate_const, orders, stoich):
        species, slabs, depth, width = conc.shape
        reactions = orders.shape[0]
        assert slabs == 1
        kinds, relays = [[CHAIN] * (depth + 1)] * 2, [[(r, range(sizes[0])) for r in range(depth + 1)]] * 2
        if sizes[0] <= 4 and depth == 4:
            kinds, relays = [[PAIR,RELAY,PAIR,PAIR,PAIR],[PAIR,RELAY,PAIR,PAIR,PAIR]], [[(r, [q]) for r, q in steps] for steps in [[(2, 1), (3, 1), (1, 2), (4, 1), (0, 1)], [(2, 1), (3, 1), (1, 2), (0, 1), (4, 1)]]]
        span = max(max([0, *raw, *led]) for row_kinds in kinds for raw, led in (plan(kind, sizes[0]) for kind in row_kinds)) or 1
        block = (depth, species, width)
        more = (depth + 1, species, width)
        one = (species, width)
        hbm = pl.BlockSpec(memory_space=pltpu.HBM)
        vmem = pl.BlockSpec(memory_space=pltpu.VMEM)
        cells = depth * width
        dma = pltpu.SemaphoreType.DMA
        outs = pl.pallas_call(
            functools.partial(kernel, sizes, kinds, relays),
            name="flame_adjoint",
            out_shape=jax.ShapeDtypeStruct((2, species, 1, depth, width), F32),
            in_specs=[hbm] * 7,
            out_specs=vmem,
            scratch_shapes=[
                pltpu.VMEM(block, F32), pltpu.VMEM(block, F32), pltpu.VMEM(more, F32), pltpu.VMEM(block, F32), pltpu.VMEM(block, F32),
                pltpu.VMEM((4,) + more, F32), pltpu.VMEM((4,) + one, F32),
                pltpu.VMEM((2, 2) + block, F32), pltpu.VMEM((2, 2) + one, F32), pltpu.VMEM((2, 2) + more, F32),
                pltpu.VMEM((2, 2, depth + 1, span) + one, F32),
                pltpu.VMEM((8, width), F32), pltpu.VMEM((8, width), F32),
                pltpu.VMEM((depth, width), F32), pltpu.VMEM((depth, width), jnp.int32), pltpu.VMEM((1, reactions), F32),
                pltpu.VMEM((reactions, cells), F32), pltpu.VMEM((reactions, cells + width), F32),
                pltpu.VMEM((2, reactions, cells + width), BF16), pltpu.VMEM((2, reactions, cells), BF16),
                pltpu.VMEM((species, reactions), jnp.int32), pltpu.VMEM((species, reactions), jnp.int32),
                pltpu.VMEM((reactions, 2 * species), BF16), pltpu.VMEM((species, reactions), BF16),
                pltpu.VMEM((reactions, 2 * species), BF16), pltpu.VMEM((species, reactions), BF16),
                pltpu.VMEM((reactions, width), F32),
                dma((2, depth)), dma((5,)),
                dma((2, 2, depth, span)), dma((2, 2, span + 1)), dma((2, 2, depth + 1, span)),
                dma((2, 2, depth + 1, span)), dma((2, 2)), dma((6,)), dma((6,)),
            ],
            compiler_params=pltpu.CompilerParams(collective_id=0, has_side_effects=True, vmem_limit_bytes=48 * 1024 * 1024),
        )(*[pltpu.with_memory_space_constraint(a, pltpu.HBM) for a in (conc, cotangent, courant, direction, rate_const.reshape(1, reactions), orders.T, stoich)])
        return outs[0], outs[1]

    placed = (
        P(None, ("grp", "gx"), ("gy", "row"), None),
        P(None, ("grp", "gx"), ("gy", "row"), None),
        P(("grp", "gy", "row"), None),
        P(("grp", "gy", "row"), None),
        P(),
        P(),
        P(),
    )
    return jax.shard_map(
        shards,
        mesh=mesh,
        in_specs=placed,
        out_specs=(P(None, ("grp", "gx"), ("gy", "row"), None),) * 2,
        check_vma=False,
    )
```

```python
import functools

import jax
import jax.numpy as jnp
from jax import lax
from jax.experimental import pallas as pl
from jax.experimental.pallas import tpu as pltpu
from jax.sharding import PartitionSpec as P

MESH = pl.DeviceIdType.MESH
F32 = jnp.float32
BF16 = jnp.bfloat16
TIME_STEP = 0.1
DIFFUSION = 0.1
HALF_LOG2E = 0.5 * 1.4426950408889634
STAR0, CARRY1, STAR1, CARRY0 = range(4)
DIRECT, RELAY, PAIR, CHAIN = (0, 1, 2, 3), (0, 1, 2, 0), (0, 1, 0, 1), (0, 1, 0, 0)


def plan(kind, nx):
    raw, led = {}, {}
    for q in range(1, nx):
        count = kind[q] if q < len(kind) else 0
        for k in range(1, count + 1):
            raw.setdefault(k, []).append(q)
        if count < q:
            led.setdefault(count + 1, []).append(q)
    return raw, led


def member(q, places):
    found, places = None, sorted(places)
    while places:
        size = 1
        while size < len(places) and places[size] == places[0] + size:
            size += 1
        run = (q >= places[0]) & (q <= places[size - 1])
        found = run if found is None else found | run
        places = places[size:]
    return found


def kernel(
    sizes, kinds, relays, conc_hbm, cot_hbm, cour_hbm, dir_hbm, const_hbm, ord_hbm, sto_hbm, out,
    conc, cot, state, spread, lam, field, sib, mixed, mixed_h, swept, recv, aux_out, aux_in,
    cour_v, dir_v, const_v, rates0, rates1, rates_b, grad_b,
    ord_i, sto_i, ord2, ord_t, sto2, sto, log_k,
    in_sem, tab_sem, send_sem, dsend_sem, recv_sem, lsend_sem, wrecv_sem, esend_sem, erecv_sem,
):
    nx, ngy, nrow = sizes
    depth, species, width = conc.shape
    halo = depth
    reactions = ord_i.shape[1]
    late = [1, 0] if depth > 1 else [0]
    early = [list(range(r, min(r + 2, depth))) for r in range(2, depth, 2)]
    ends = sorted({0, depth - 1})
    inner = list(range(1, depth - 1))
    order = [r for rows in early for r in rows] + late + [halo]
    spots = {STAR0: ends + inner, STAR1: order}
    chunk = min(256, reactions)
    plans = [[plan(kind, nx) for kind in row_kinds] for row_kinds in kinds]
    spans = [[max([0, *raw, *led]) for raw, led in row_plans] for row_plans in plans]

    x = lax.axis_index("gx")
    gy = lax.axis_index("gy")
    row = lax.axis_index("row")
    q_of = [x, nx - 1 - x]
    there = jnp.where(row == 0, gy > 0, gy < ngy - 1)
    across = {"gy": gy + 2 * row - 1, "row": 1 - row}
    beside = {"row": 1 - row}

    def place(r):
        return r + row * (depth - 1 - 2 * r)

    def load(source, target, base):
        return [pltpu.make_async_copy(source.at[:, 0, r, :], target.at[place(r)], in_sem.at[base, r]) for r in range(depth)]

    loads_conc = load(conc_hbm, conc, 0)
    loads_cot = load(cot_hbm, cot, 1)
    tables = [pltpu.make_async_copy(a, b, tab_sem.at[i]) for i, (a, b) in enumerate(
        ((ord_hbm, ord_i), (sto_hbm, sto_i), (const_hbm, const_v), (cour_hbm, cour_v), (dir_hbm, dir_v)))]
    for copy in tables + loads_conc:
        copy.start()

    def inside(target):
        return (target >= 0) & (target < nx)

    own_span = max(max(row_spans) for row_spans in spans)
    halo_span = max(max([0, *row_plans[halo][0]]) for row_plans in plans)
    partners = [(None, beside)]
    for k in range(1, max(own_span, halo_span) + 1):
        for sign in (1, -1):
            partners.append((inside(x + sign * k), {"gx": x + sign * k}))
    partners.append((there, across))
    for k in range(1, halo_span + 1):
        for sign in (1, -1):
            partners.append((there & inside(x + sign * k), {"gx": x + sign * k, **across}))

    def when(condition, action):
        if condition is None:
            action()
        else:
            pl.when(condition)(action)

    barrier = pltpu.get_barrier_semaphore()
    for condition, device in partners:
        when(condition, lambda: pl.semaphore_signal(barrier, inc=1, device_id=device, device_id_type=MESH))

    for copy in loads_cot:
        copy.start()

    def nothing(ref, *index):
        ref[index] = jnp.zeros_like(ref[index])

    for d in range(2):
        missing = {}
        for p in range(2):
            for r in range(depth + 1):
                raw, led = plans[p][r]
                for k in range(1, spans[p][r] + 1):
                    missing.setdefault((r == halo, *sorted(raw.get(k, []) + led.get(k, []))), []).append((p, d, r, k - 1))
        for (outer, *places), slots in missing.items():
            got = member(q_of[d], places)

            @pl.when(jnp.logical_not(got & there if outer else got))
            def _():
                for slot in slots:
                    nothing(recv, *slot)

    @pl.when(jnp.logical_not(there))
    def _():
        nothing(field, STAR0, halo)
        nothing(aux_in, slice(None))
        for p in range(2):
            for d in range(2):
                nothing(mixed_h, p, d)

    for copy in tables:
        copy.wait()

    def pick(ref, r):
        return jnp.where(row == 0, ref[r:r + 1], ref[depth - 1 - r:depth - r])

    courant = [pick(cour_v, r) for r in range(depth)]
    upward = [pick(dir_v, r).astype(F32) for r in range(depth)]
    aux_out[...] = jnp.zeros_like(aux_out)
    aux_out[0:1] = courant[0]
    aux_out[1:2] = upward[0]
    retain = [c / (1.0 + c) for c in courant]
    admit = [1.0 / (1.0 + c) for c in courant]
    rising = [jnp.broadcast_to(u, (species, width)) > 0.5 for u in upward]

    order_float = ord_i[...].astype(F32)
    order_trans = order_float.T.astype(BF16)
    ord2[:, :species] = order_trans
    ord2[:, species:] = order_trans
    stoich_float = sto_i[...].astype(F32)
    sto[...] = stoich_float.astype(BF16)
    log_k[...] = jnp.broadcast_to(jnp.log(const_v[...]) * (2.0 * HALF_LOG2E), (width, reactions)).T
    for copy in loads_conc:
        copy.wait()

    drains = []

    def begin(condition, make):
        when(condition, lambda: make().start())
        drains.append((condition, make))

    def drain():
        for condition, make in drains:
            when(condition, lambda: make().wait_send())
        drains.clear()

    def along(p, d, r, k, source, swept_value):
        return pltpu.make_async_remote_copy(
            src_ref=source, dst_ref=recv.at[p, d, r, k - 1],
            send_sem=(lsend_sem if swept_value else send_sem).at[p, d, r, k - 1], recv_sem=recv_sem.at[p, d, r, k - 1],
            device_id={"gx": x + k * (1 - 2 * d)}, device_id_type=MESH)

    def aslant(p, d, k):
        return pltpu.make_async_remote_copy(
            src_ref=mixed.at[p, d, 0], dst_ref=mixed_h.at[p, d] if k == 0 else recv.at[p, d, halo, k - 1],
            send_sem=dsend_sem.at[p, d, k], recv_sem=wrecv_sem.at[p, d] if k == 0 else recv_sem.at[p, d, halo, k - 1],
            device_id={"gx": x + k * (1 - 2 * d), **across} if k else across, device_id_type=MESH)

    def send_raw(p, r):
        for k in sorted(plans[p][r][0], reverse=True):
            for d in range(2):
                begin(member(q_of[d], [q - k for q in plans[p][r][0][k]]), functools.partial(along, p, d, r, k, mixed.at[p, d, r], False))

    def send_aslant(p):
        for k in sorted(plans[p][halo][0], reverse=True):
            for d in range(2):
                begin(there & member(q_of[d], [q - k for q in plans[p][halo][0][k]]), functools.partial(aslant, p, d, k))
        for d in range(2):
            begin(there, functools.partial(aslant, p, d, 0))

    def arrivals(p, d, r):
        raw, led = plans[p][r]
        if r == halo:
            yield there, aslant(p, d, 0)
        for k in range(1, spans[p][r] + 1):
            for table in (raw, led):
                if k in table:
                    got = member(q_of[d], table[k])
                    yield got & there if r == halo and table is raw else got, along(p, d, r, k, recv.at[p, d, r, k - 1], False)

    def passing(p, r, places=None):
        return [q - k for k, got in plans[p][r][1].items() for q in got if places is None or q - k in places]

    def total(p, d, r):
        value = mixed_h[p, d] if r == halo else mixed[p, d, r]
        carried = None
        for k in range(spans[p][r], 0, -1):
            carried = recv[p, d, r, k - 1] if carried is None else recv[p, d, r, k - 1] + retain[r] * carried
        return value if carried is None else value + retain[r] * carried

    def relay(p, r, places):
        for d in range(2):
            if not passing(p, r, places):
                continue

            @pl.when(member(q_of[d], passing(p, r, places)))
            def _():
                for got, copy in arrivals(p, d, r):
                    pl.when(got)(copy.wait_recv)
                swept[p, d, r] = total(p, d, r)
            for k, got in plans[p][r][1].items():
                senders = [q - k for q in got if q - k in places]
                if senders:
                    begin(member(q_of[d], senders), functools.partial(along, p, d, r, k, swept.at[p, d, r], True))

    def collect(p, r):
        for d in range(2):
            for got, copy in arrivals(p, d, r):
                if passing(p, r):
                    got = got & jnp.logical_not(member(q_of[d], passing(p, r)))
                pl.when(got)(copy.wait_recv)
        ahead, back = total(p, 0, r), total(p, 1, r)
        return jnp.where(rising[r], ahead, back), jnp.where(rising[r], back, ahead)

    def edge_copy(k):
        if k < 4:
            return pltpu.make_async_remote_copy(
                src_ref=field.at[k, depth - 1], dst_ref=sib.at[k], send_sem=esend_sem.at[k], recv_sem=erecv_sem.at[k],
                device_id=beside, device_id_type=MESH)
        source, target = ((field.at[STAR0, 0], field.at[STAR0, halo]), (aux_out, aux_in))[k - 4]
        return pltpu.make_async_remote_copy(
            src_ref=source, dst_ref=target, send_sem=esend_sem.at[k], recv_sem=erecv_sem.at[k],
            device_id=across, device_id_type=MESH)

    def edge_send(k):
        begin(None if k < 4 else there, functools.partial(edge_copy, k))

    def edge_wait(k):
        when(None if k < 4 else there, lambda: edge_copy(k).wait_recv())

    lane = lax.broadcasted_iota(jnp.int32, (species, width), 1)

    def smooth(k, r):
        here = field[k, r]
        below = field[k, halo] if r == 0 else field[k, r - 1]
        above = sib[k] if r == depth - 1 else field[k, r + 1]
        before = jnp.where(lane == 0, 0.0, pltpu.roll(here, 1, 1))
        after = jnp.where(lane == width - 1, 0.0, pltpu.roll(here, width - 1, 1))
        return here + DIFFUSION * (above + below + after + before - 4.0 * here)

    def side(parts):
        return parts[0] if len(parts) == 1 else jnp.concatenate(parts, axis=1)

    def split(value):
        high = value.astype(BF16)
        low = (value - high.astype(F32)).astype(BF16)
        return jnp.concatenate([high, low], axis=0)

    parts = [pl.ds(i, chunk) for i in range(0, reactions, chunk)]

    def keep(target, part, cols, value):
        high = value.astype(BF16)
        target[0, part, cols] = high
        target[1, part, cols] = (value - high.astype(F32)).astype(BF16)

    def gather(table, part, value, so_far):
        high = value.astype(BF16)
        low = (value - high.astype(F32)).astype(BF16)
        small = jnp.dot(table[:, part], low, preferred_element_type=F32)
        both = small + jnp.dot(table[:, part], high, preferred_element_type=F32)
        return both if so_far is None else so_far + both

    def columns(listed, rows):
        return pl.ds(listed.index(rows[0]) * width, len(rows) * width)

    def react(rows, source, rates_ref, k):
        act, cols = split(side([HALF_LOG2E * jnp.log(1.0 + source[r] * source[r]) for r in rows])), columns(spots[k], rows)
        produced = None
        for part in parts:
            exponent = jnp.dot(ord2[part, :], act, preferred_element_type=F32)
            rates = jnp.exp2(exponent + side([log_k[part, :]] * len(rows)))
            rates_ref[part, cols] = rates
            produced = gather(sto, part, rates, produced)
        for i, r in enumerate(rows):
            value = source[r] + TIME_STEP * produced[:, i * width:(i + 1) * width]
            field[k, r] = jnp.where(there, value, 0.0) if r == halo else value

    def react_back(rows, cells, rates_ref, k, put):
        cols = columns(order, rows)
        push = split(side([spread[r] for r in rows]))
        summed = None
        for part in parts:
            pulled = jnp.dot(sto2[part, :], push, preferred_element_type=F32)
            summed = gather(ord_t, part, side([rates_ref[part, columns(spots[k], [r])] for r in rows]) * pulled, summed)
        for i, r in enumerate(rows):
            c = cells[r]
            put(r, spread[r] + TIME_STEP * c / (1.0 + c * c) * summed[:, i * width:(i + 1) * width])

    def mix(p, k, r, back):
        ahead = admit[r] * smooth(k, r)
        mixed[p, 0, r] = jnp.where(rising[r], ahead, back[r])
        mixed[p, 1, r] = jnp.where(rising[r], back[r], ahead)

    def put(target, r, value):
        for side_row in range(2):
            @pl.when(row == side_row)
            def _():
                out[target, :, 0, depth - 1 - r if side_row else r, :] = value

    def put_lam(r, value):
        lam[r] = value

    def put_out(r, value):
        put(1, r, value)

    last = depth - 1

    react(ends, conc, rates0, STAR0)
    pl.semaphore_wait(barrier, sum(1 if c is None else jnp.where(c, 1, 0) for c, _ in partners))
    edge_send(4)
    edge_send(STAR0)
    edge_send(5)
    for i in range(0, len(inner), 2):
        react(inner[i:i + 2], conc, rates0, STAR0)
    for copy in loads_cot:
        copy.wait()
    edge_wait(STAR0)
    for r in [*range(2, depth), 1][:last]:
        mix(0, STAR0, r, cot)
        send_raw(0, r)
    ord_t[...] = ord_i[...].astype(F32).astype(BF16)
    stoich_trans = sto_i[...].astype(F32).T.astype(BF16)
    sto2[:, :species] = stoich_trans
    sto2[:, species:] = stoich_trans
    edge_wait(4)
    mix(0, STAR0, 0, cot)
    send_aslant(0)
    send_raw(0, 0)
    edge_wait(5)
    retain.append(aux_in[0:1] / (1.0 + aux_in[0:1]))
    admit.append(1.0 / (1.0 + aux_in[0:1]))
    rising.append(jnp.broadcast_to(aux_in[1:2], (species, width)) > 0.5)
    for r, places in relays[0]:
        relay(0, r, places)

    def gain(r):
        ahead, back = collect(0, r)
        state[r] = ahead
        field[CARRY1, r] = admit[r] * back

    for rows in early:
        for r in rows:
            gain(r)
        if last in rows:
            edge_send(CARRY1)
        react(rows, state, rates1, STAR1)
    if last > 1:
        edge_send(STAR1)
    if depth > 1:
        gain(1)
        if last == 1:
            edge_send(CARRY1)
        react([1], state, rates1, STAR1)
        if last == 1:
            edge_send(STAR1)
    for rows in early:
        for r in rows:
            if r == last:
                edge_wait(CARRY1)
            spread[r] = smooth(CARRY1, r)
        react_back(rows, state, rates1, STAR1, put_lam)
    marked = len(drains)
    for rows in early:
        for r in rows:
            if r == last:
                edge_wait(STAR1)
            mix(1, STAR1, r, lam)
            send_raw(1, r)
    gain(0)
    gain(halo)
    if last == 0:
        edge_send(CARRY1)
    react([0, halo], state, rates1, STAR1)
    if last == 0:
        edge_send(STAR1)
    for r in late:
        if r == last:
            edge_wait(CARRY1)
        spread[r] = smooth(CARRY1, r)
    react_back(late, state, rates1, STAR1, put_lam)
    for r in late:
        if r == last:
            edge_wait(STAR1)
        mix(1, STAR1, r, lam)
        if r == 0:
            send_aslant(1)
        send_raw(1, r)
    for r, places in relays[1]:
        relay(1, r, places)

    drain_late = drains[marked:]
    del drains[marked:]
    drain()
    drains.extend(drain_late)

    def finish(r):
        ahead, back = collect(1, r)
        if r != halo:
            put(0, r, ahead)
        field[CARRY0, r] = admit[r] * back
        if r == last:
            edge_send(CARRY0)

    for rows in early:
        for r in rows:
            finish(r)
    for r in late:
        if r:
            finish(r)
    for rows in early:
        for r in rows:
            if r == last:
                edge_wait(CARRY0)
            spread[r] = smooth(CARRY0, r)
        react_back(rows, conc, rates0, STAR0, put_out)
    drain()
    finish(0)
    finish(halo)
    for r in late:
        if r == last:
            edge_wait(CARRY0)
        spread[r] = smooth(CARRY0, r)
    react_back(late, conc, rates0, STAR0, put_out)

    drain()


def solution(mesh):
    sizes = (mesh.shape["gx"], mesh.shape["gy"], mesh.shape["row"])
    assert sizes[2] == 2

    def shards(conc, cotangent, courant, direction, rate_const, orders, stoich):
        species, slabs, depth, width = conc.shape
        reactions = orders.shape[0]
        assert slabs == 1
        kinds, relays = [[CHAIN] * (depth + 1)] * 2, [[(r, range(sizes[0])) for r in range(depth + 1)]] * 2
        if sizes[0] <= 4 and depth == 4:
            kinds, relays = [[PAIR,RELAY,PAIR,PAIR,PAIR],[PAIR,PAIR,PAIR,RELAY,RELAY]], [[(r, [q]) for r, q in steps] for steps in [[(2, 1), (3, 1), (1, 2), (4, 1), (0, 1)], [(2, 1), (3, 2), (1, 1), (4, 2), (0, 1)]]]
        span = max(max([0, *raw, *led]) for row_kinds in kinds for raw, led in (plan(kind, sizes[0]) for kind in row_kinds)) or 1
        block = (depth, species, width)
        more = (depth + 1, species, width)
        one = (species, width)
        hbm = pl.BlockSpec(memory_space=pltpu.HBM)
        vmem = pl.BlockSpec(memory_space=pltpu.VMEM)
        cells = depth * width
        dma = pltpu.SemaphoreType.DMA
        outs = pl.pallas_call(
            functools.partial(kernel, sizes, kinds, relays),
            name="flame_adjoint",
            out_shape=jax.ShapeDtypeStruct((2, species, 1, depth, width), F32),
            in_specs=[hbm] * 7,
            out_specs=vmem,
            scratch_shapes=[
                pltpu.VMEM(block, F32), pltpu.VMEM(block, F32), pltpu.VMEM(more, F32), pltpu.VMEM(block, F32), pltpu.VMEM(block, F32),
                pltpu.VMEM((4,) + more, F32), pltpu.VMEM((4,) + one, F32),
                pltpu.VMEM((2, 2) + block, F32), pltpu.VMEM((2, 2) + one, F32), pltpu.VMEM((2, 2) + more, F32),
                pltpu.VMEM((2, 2, depth + 1, span) + one, F32),
                pltpu.VMEM((8, width), F32), pltpu.VMEM((8, width), F32),
                pltpu.VMEM((depth, width), F32), pltpu.VMEM((depth, width), jnp.int32), pltpu.VMEM((1, reactions), F32),
                pltpu.VMEM((reactions, cells), F32), pltpu.VMEM((reactions, cells + width), F32),
                pltpu.VMEM((2, reactions, cells + width), BF16), pltpu.VMEM((2, reactions, cells), BF16),
                pltpu.VMEM((species, reactions), jnp.int32), pltpu.VMEM((species, reactions), jnp.int32),
                pltpu.VMEM((reactions, 2 * species), BF16), pltpu.VMEM((species, reactions), BF16),
                pltpu.VMEM((reactions, 2 * species), BF16), pltpu.VMEM((species, reactions), BF16),
                pltpu.VMEM((reactions, width), F32),
                dma((2, depth)), dma((5,)),
                dma((2, 2, depth, span)), dma((2, 2, span + 1)), dma((2, 2, depth + 1, span)),
                dma((2, 2, depth + 1, span)), dma((2, 2)), dma((6,)), dma((6,)),
            ],
            compiler_params=pltpu.CompilerParams(collective_id=0, has_side_effects=True, vmem_limit_bytes=48 * 1024 * 1024),
        )(*[pltpu.with_memory_space_constraint(a, pltpu.HBM) for a in (conc, cotangent, courant, direction, rate_const.reshape(1, reactions), orders.T, stoich)])
        return outs[0], outs[1]

    placed = (
        P(None, ("grp", "gx"), ("gy", "row"), None),
        P(None, ("grp", "gx"), ("gy", "row"), None),
        P(("grp", "gy", "row"), None),
        P(("grp", "gy", "row"), None),
        P(),
        P(),
        P(),
    )
    return jax.shard_map(
        shards,
        mesh=mesh,
        in_specs=placed,
        out_specs=(P(None, ("grp", "gx"), ("gy", "row"), None),) * 2,
        check_vma=False,
    )
```

```python
import functools

import jax
import jax.numpy as jnp
from jax import lax
from jax.experimental import pallas as pl
from jax.experimental.pallas import tpu as pltpu
from jax.sharding import PartitionSpec as P

MESH = pl.DeviceIdType.MESH
F32 = jnp.float32
BF16 = jnp.bfloat16
TIME_STEP = 0.1
DIFFUSION = 0.1
HALF_LOG2E = 0.5 * 1.4426950408889634
STAR0, CARRY1, STAR1, CARRY0 = range(4)
DIRECT, RELAY, PAIR, CHAIN = (0, 1, 2, 3), (0, 1, 2, 0), (0, 1, 0, 1), (0, 1, 0, 0)


def plan(kind, nx):
    raw, led = {}, {}
    for q in range(1, nx):
        count = kind[q] if q < len(kind) else 0
        for k in range(1, count + 1):
            raw.setdefault(k, []).append(q)
        if count < q:
            led.setdefault(count + 1, []).append(q)
    return raw, led


def member(q, places):
    found, places = None, sorted(places)
    while places:
        size = 1
        while size < len(places) and places[size] == places[0] + size:
            size += 1
        run = (q >= places[0]) & (q <= places[size - 1])
        found = run if found is None else found | run
        places = places[size:]
    return found


def kernel(
    sizes, kinds, relays, conc_hbm, cot_hbm, cour_hbm, dir_hbm, const_hbm, ord_hbm, sto_hbm, out,
    conc, cot, state, spread, lam, field, sib, mixed, mixed_h, swept, recv, aux_out, aux_in,
    cour_v, dir_v, const_v, rates0, rates1, rates_b, grad_b,
    ord_i, sto_i, ord2, ord_t, sto2, sto, log_k,
    in_sem, tab_sem, send_sem, dsend_sem, recv_sem, lsend_sem, wrecv_sem, esend_sem, erecv_sem,
):
    nx, ngy, nrow = sizes
    depth, species, width = conc.shape
    halo = depth
    reactions = ord_i.shape[1]
    late = [1, 0] if depth > 1 else [0]
    early = [list(range(r, min(r + 2, depth))) for r in range(2, depth, 2)]
    ends = sorted({0, depth - 1})
    inner = list(range(1, depth - 1))
    order = [r for rows in early for r in rows] + late + [halo]
    spots = {STAR0: ends + inner, STAR1: order}
    chunk = min(256, reactions)
    plans = [[plan(kind, nx) for kind in row_kinds] for row_kinds in kinds]
    spans = [[max([0, *raw, *led]) for raw, led in row_plans] for row_plans in plans]

    x = lax.axis_index("gx")
    gy = lax.axis_index("gy")
    row = lax.axis_index("row")
    q_of = [x, nx - 1 - x]
    there = jnp.where(row == 0, gy > 0, gy < ngy - 1)
    across = {"gy": gy + 2 * row - 1, "row": 1 - row}
    beside = {"row": 1 - row}

    def place(r):
        return r + row * (depth - 1 - 2 * r)

    def load(source, target, base):
        return [pltpu.make_async_copy(source.at[:, 0, r, :], target.at[place(r)], in_sem.at[base, r]) for r in range(depth)]

    loads_conc = load(conc_hbm, conc, 0)
    loads_cot = load(cot_hbm, cot, 1)
    tables = [pltpu.make_async_copy(a, b, tab_sem.at[i]) for i, (a, b) in enumerate(
        ((ord_hbm, ord_i), (sto_hbm, sto_i), (const_hbm, const_v), (cour_hbm, cour_v), (dir_hbm, dir_v)))]
    for copy in tables + loads_conc:
        copy.start()

    def inside(target):
        return (target >= 0) & (target < nx)

    own_span = max(max(row_spans) for row_spans in spans)
    halo_span = max(max([0, *row_plans[halo][0]]) for row_plans in plans)
    partners = [(None, beside)]
    for k in range(1, max(own_span, halo_span) + 1):
        for sign in (1, -1):
            partners.append((inside(x + sign * k), {"gx": x + sign * k}))
    partners.append((there, across))
    for k in range(1, halo_span + 1):
        for sign in (1, -1):
            partners.append((there & inside(x + sign * k), {"gx": x + sign * k, **across}))

    def when(condition, action):
        if condition is None:
            action()
        else:
            pl.when(condition)(action)

    barrier = pltpu.get_barrier_semaphore()
    for condition, device in partners:
        when(condition, lambda: pl.semaphore_signal(barrier, inc=1, device_id=device, device_id_type=MESH))

    for copy in loads_cot:
        copy.start()

    def nothing(ref, *index):
        ref[index] = jnp.zeros_like(ref[index])

    for d in range(2):
        missing = {}
        for p in range(2):
            for r in range(depth + 1):
                raw, led = plans[p][r]
                for k in range(1, spans[p][r] + 1):
                    missing.setdefault((r == halo, *sorted(raw.get(k, []) + led.get(k, []))), []).append((p, d, r, k - 1))
        for (outer, *places), slots in missing.items():
            got = member(q_of[d], places)

            @pl.when(jnp.logical_not(got & there if outer else got))
            def _():
                for slot in slots:
                    nothing(recv, *slot)

    @pl.when(jnp.logical_not(there))
    def _():
        nothing(field, STAR0, halo)
        nothing(aux_in, slice(None))
        for p in range(2):
            for d in range(2):
                nothing(mixed_h, p, d)

    for copy in tables:
        copy.wait()

    def pick(ref, r):
        return jnp.where(row == 0, ref[r:r + 1], ref[depth - 1 - r:depth - r])

    courant = [pick(cour_v, r) for r in range(depth)]
    upward = [pick(dir_v, r).astype(F32) for r in range(depth)]
    aux_out[...] = jnp.zeros_like(aux_out)
    aux_out[0:1] = courant[0]
    aux_out[1:2] = upward[0]
    retain = [c / (1.0 + c) for c in courant]
    admit = [1.0 / (1.0 + c) for c in courant]
    rising = [jnp.broadcast_to(u, (species, width)) > 0.5 for u in upward]

    order_float = ord_i[...].astype(F32)
    order_trans = order_float.T.astype(BF16)
    ord2[:, :species] = order_trans
    ord2[:, species:] = order_trans
    stoich_float = sto_i[...].astype(F32)
    sto[...] = stoich_float.astype(BF16)
    log_k[...] = jnp.broadcast_to(jnp.log(const_v[...]) * (2.0 * HALF_LOG2E), (width, reactions)).T
    for copy in loads_conc:
        copy.wait()

    drains = []

    def begin(condition, make):
        when(condition, lambda: make().start())
        drains.append((condition, make))

    def drain():
        for condition, make in drains:
            when(condition, lambda: make().wait_send())
        drains.clear()

    def along(p, d, r, k, source, swept_value):
        return pltpu.make_async_remote_copy(
            src_ref=source, dst_ref=recv.at[p, d, r, k - 1],
            send_sem=(lsend_sem if swept_value else send_sem).at[p, d, r, k - 1], recv_sem=recv_sem.at[p, d, r, k - 1],
            device_id={"gx": x + k * (1 - 2 * d)}, device_id_type=MESH)

    def aslant(p, d, k):
        return pltpu.make_async_remote_copy(
            src_ref=mixed.at[p, d, 0], dst_ref=mixed_h.at[p, d] if k == 0 else recv.at[p, d, halo, k - 1],
            send_sem=dsend_sem.at[p, d, k], recv_sem=wrecv_sem.at[p, d] if k == 0 else recv_sem.at[p, d, halo, k - 1],
            device_id={"gx": x + k * (1 - 2 * d), **across} if k else across, device_id_type=MESH)

    def send_raw(p, r):
        for k in sorted(plans[p][r][0], reverse=True):
            for d in range(2):
                begin(member(q_of[d], [q - k for q in plans[p][r][0][k]]), functools.partial(along, p, d, r, k, mixed.at[p, d, r], False))

    def send_aslant(p):
        for k in sorted(plans[p][halo][0], reverse=True):
            for d in range(2):
                begin(there & member(q_of[d], [q - k for q in plans[p][halo][0][k]]), functools.partial(aslant, p, d, k))
        for d in range(2):
            begin(there, functools.partial(aslant, p, d, 0))

    def arrivals(p, d, r):
        raw, led = plans[p][r]
        if r == halo:
            yield there, aslant(p, d, 0)
        for k in range(1, spans[p][r] + 1):
            for table in (raw, led):
                if k in table:
                    got = member(q_of[d], table[k])
                    yield got & there if r == halo and table is raw else got, along(p, d, r, k, recv.at[p, d, r, k - 1], False)

    def passing(p, r, places=None):
        return [q - k for k, got in plans[p][r][1].items() for q in got if places is None or q - k in places]

    def total(p, d, r):
        value = mixed_h[p, d] if r == halo else mixed[p, d, r]
        carried = None
        for k in range(spans[p][r], 0, -1):
            carried = recv[p, d, r, k - 1] if carried is None else recv[p, d, r, k - 1] + retain[r] * carried
        return value if carried is None else value + retain[r] * carried

    def relay(p, r, places):
        for d in range(2):
            if not passing(p, r, places):
                continue

            @pl.when(member(q_of[d], passing(p, r, places)))
            def _():
                for got, copy in arrivals(p, d, r):
                    pl.when(got)(copy.wait_recv)
                swept[p, d, r] = total(p, d, r)
            for k, got in plans[p][r][1].items():
                senders = [q - k for q in got if q - k in places]
                if senders:
                    begin(member(q_of[d], senders), functools.partial(along, p, d, r, k, swept.at[p, d, r], True))

    def collect(p, r):
        for d in range(2):
            for got, copy in arrivals(p, d, r):
                if passing(p, r):
                    got = got & jnp.logical_not(member(q_of[d], passing(p, r)))
                pl.when(got)(copy.wait_recv)
        ahead, back = total(p, 0, r), total(p, 1, r)
        return jnp.where(rising[r], ahead, back), jnp.where(rising[r], back, ahead)

    def edge_copy(k):
        if k < 4:
            return pltpu.make_async_remote_copy(
                src_ref=field.at[k, depth - 1], dst_ref=sib.at[k], send_sem=esend_sem.at[k], recv_sem=erecv_sem.at[k],
                device_id=beside, device_id_type=MESH)
        source, target = ((field.at[STAR0, 0], field.at[STAR0, halo]), (aux_out, aux_in))[k - 4]
        return pltpu.make_async_remote_copy(
            src_ref=source, dst_ref=target, send_sem=esend_sem.at[k], recv_sem=erecv_sem.at[k],
            device_id=across, device_id_type=MESH)

    def edge_send(k):
        begin(None if k < 4 else there, functools.partial(edge_copy, k))

    def edge_wait(k):
        when(None if k < 4 else there, lambda: edge_copy(k).wait_recv())

    lane = lax.broadcasted_iota(jnp.int32, (species, width), 1)

    def smooth(k, r):
        here = field[k, r]
        below = field[k, halo] if r == 0 else field[k, r - 1]
        above = sib[k] if r == depth - 1 else field[k, r + 1]
        before = jnp.where(lane == 0, 0.0, pltpu.roll(here, 1, 1))
        after = jnp.where(lane == width - 1, 0.0, pltpu.roll(here, width - 1, 1))
        return here + DIFFUSION * (above + below + after + before - 4.0 * here)

    def side(parts):
        return parts[0] if len(parts) == 1 else jnp.concatenate(parts, axis=1)

    def split(value):
        high = value.astype(BF16)
        low = (value - high.astype(F32)).astype(BF16)
        return jnp.concatenate([high, low], axis=0)

    parts = [pl.ds(i, chunk) for i in range(0, reactions, chunk)]

    def keep(target, part, cols, value):
        high = value.astype(BF16)
        target[0, part, cols] = high
        target[1, part, cols] = (value - high.astype(F32)).astype(BF16)

    def gather(table, part, value, so_far):
        high = value.astype(BF16)
        low = (value - high.astype(F32)).astype(BF16)
        small = jnp.dot(table[:, part], low, preferred_element_type=F32)
        both = small + jnp.dot(table[:, part], high, preferred_element_type=F32)
        return both if so_far is None else so_far + both

    def columns(listed, rows):
        return pl.ds(listed.index(rows[0]) * width, len(rows) * width)

    def react(rows, source, rates_ref, k):
        act, cols = split(side([HALF_LOG2E * jnp.log(1.0 + source[r] * source[r]) for r in rows])), columns(spots[k], rows)
        produced = None
        for part in parts:
            exponent = jnp.dot(ord2[part, :], act, preferred_element_type=F32)
            rates = jnp.exp2(exponent + side([log_k[part, :]] * len(rows)))
            rates_ref[part, cols] = rates
            produced = gather(sto, part, rates, produced)
        for i, r in enumerate(rows):
            value = source[r] + TIME_STEP * produced[:, i * width:(i + 1) * width]
            field[k, r] = jnp.where(there, value, 0.0) if r == halo else value

    def react_back(rows, cells, rates_ref, k, put):
        cols = columns(order, rows)
        push = split(side([spread[r] for r in rows]))
        summed = None
        for part in parts:
            pulled = jnp.dot(sto2[part, :], push, preferred_element_type=F32)
            summed = gather(ord_t, part, side([rates_ref[part, columns(spots[k], [r])] for r in rows]) * pulled, summed)
        for i, r in enumerate(rows):
            c = cells[r]
            put(r, spread[r] + TIME_STEP * c / (1.0 + c * c) * summed[:, i * width:(i + 1) * width])

    def mix(p, k, r, back):
        ahead = admit[r] * smooth(k, r)
        mixed[p, 0, r] = jnp.where(rising[r], ahead, back[r])
        mixed[p, 1, r] = jnp.where(rising[r], back[r], ahead)

    def put(target, r, value):
        for side_row in range(2):
            @pl.when(row == side_row)
            def _():
                out[target, :, 0, depth - 1 - r if side_row else r, :] = value

    def put_lam(r, value):
        lam[r] = value

    def put_out(r, value):
        put(1, r, value)

    last = depth - 1

    react(ends, conc, rates0, STAR0)
    pl.semaphore_wait(barrier, sum(1 if c is None else jnp.where(c, 1, 0) for c, _ in partners))
    edge_send(4)
    edge_send(STAR0)
    edge_send(5)
    for i in range(0, len(inner), 2):
        react(inner[i:i + 2], conc, rates0, STAR0)
    for copy in loads_cot:
        copy.wait()
    edge_wait(STAR0)
    for r in [*range(2, depth), 1][:last]:
        mix(0, STAR0, r, cot)
        send_raw(0, r)
    ord_t[...] = ord_i[...].astype(F32).astype(BF16)
    stoich_trans = sto_i[...].astype(F32).T.astype(BF16)
    sto2[:, :species] = stoich_trans
    sto2[:, species:] = stoich_trans
    edge_wait(4)
    mix(0, STAR0, 0, cot)
    send_aslant(0)
    send_raw(0, 0)
    edge_wait(5)
    retain.append(aux_in[0:1] / (1.0 + aux_in[0:1]))
    admit.append(1.0 / (1.0 + aux_in[0:1]))
    rising.append(jnp.broadcast_to(aux_in[1:2], (species, width)) > 0.5)
    for r, places in relays[0]:
        relay(0, r, places)

    def gain(r):
        ahead, back = collect(0, r)
        state[r] = ahead
        field[CARRY1, r] = admit[r] * back

    for rows in early:
        for r in rows:
            gain(r)
        if last in rows:
            edge_send(CARRY1)
        react(rows, state, rates1, STAR1)
    if last > 1:
        edge_send(STAR1)
    if depth > 1:
        gain(1)
        if last == 1:
            edge_send(CARRY1)
        react([1], state, rates1, STAR1)
        if last == 1:
            edge_send(STAR1)
    for rows in early:
        for r in rows:
            if r == last:
                edge_wait(CARRY1)
            spread[r] = smooth(CARRY1, r)
        react_back(rows, state, rates1, STAR1, put_lam)
    marked = len(drains)
    for rows in early:
        for r in rows:
            if r == last:
                edge_wait(STAR1)
            mix(1, STAR1, r, lam)
            send_raw(1, r)
    gain(0)
    gain(halo)
    if last == 0:
        edge_send(CARRY1)
    react([0, halo], state, rates1, STAR1)
    if last == 0:
        edge_send(STAR1)
    for r in late:
        if r == last:
            edge_wait(CARRY1)
        spread[r] = smooth(CARRY1, r)
    react_back(late, state, rates1, STAR1, put_lam)
    for r in late:
        if r == last:
            edge_wait(STAR1)
        mix(1, STAR1, r, lam)
        if r == 0:
            send_aslant(1)
        send_raw(1, r)
    for r, places in relays[1]:
        relay(1, r, places)

    drain_late = drains[marked:]
    del drains[marked:]
    drain()
    drains.extend(drain_late)

    def finish(r):
        ahead, back = collect(1, r)
        if r != halo:
            put(0, r, ahead)
        field[CARRY0, r] = admit[r] * back
        if r == last:
            edge_send(CARRY0)

    for rows in early:
        for r in rows:
            finish(r)
    for r in late:
        if r:
            finish(r)
    for rows in early:
        for r in rows:
            if r == last:
                edge_wait(CARRY0)
            spread[r] = smooth(CARRY0, r)
        react_back(rows, conc, rates0, STAR0, put_out)
    drain()
    finish(0)
    finish(halo)
    for r in late:
        if r == last:
            edge_wait(CARRY0)
        spread[r] = smooth(CARRY0, r)
    react_back(late, conc, rates0, STAR0, put_out)

    drain()


def solution(mesh):
    sizes = (mesh.shape["gx"], mesh.shape["gy"], mesh.shape["row"])
    assert sizes[2] == 2

    def shards(conc, cotangent, courant, direction, rate_const, orders, stoich):
        species, slabs, depth, width = conc.shape
        reactions = orders.shape[0]
        assert slabs == 1
        kinds, relays = [[CHAIN] * (depth + 1)] * 2, [[(r, range(sizes[0])) for r in range(depth + 1)]] * 2
        if sizes[0] <= 4 and depth == 4:
            kinds, relays = [[PAIR,RELAY,PAIR,PAIR,PAIR],[PAIR,PAIR,PAIR,PAIR,RELAY]], [[(r, [q]) for r, q in steps] for steps in [[(2, 1), (3, 1), (1, 2), (4, 1), (0, 1)], [(2, 1), (3, 1), (1, 1), (4, 2), (0, 1)]]]
        span = max(max([0, *raw, *led]) for row_kinds in kinds for raw, led in (plan(kind, sizes[0]) for kind in row_kinds)) or 1
        block = (depth, species, width)
        more = (depth + 1, species, width)
        one = (species, width)
        hbm = pl.BlockSpec(memory_space=pltpu.HBM)
        vmem = pl.BlockSpec(memory_space=pltpu.VMEM)
        cells = depth * width
        dma = pltpu.SemaphoreType.DMA
        outs = pl.pallas_call(
            functools.partial(kernel, sizes, kinds, relays),
            name="flame_adjoint",
            out_shape=jax.ShapeDtypeStruct((2, species, 1, depth, width), F32),
            in_specs=[hbm] * 7,
            out_specs=vmem,
            scratch_shapes=[
                pltpu.VMEM(block, F32), pltpu.VMEM(block, F32), pltpu.VMEM(more, F32), pltpu.VMEM(block, F32), pltpu.VMEM(block, F32),
                pltpu.VMEM((4,) + more, F32), pltpu.VMEM((4,) + one, F32),
                pltpu.VMEM((2, 2) + block, F32), pltpu.VMEM((2, 2) + one, F32), pltpu.VMEM((2, 2) + more, F32),
                pltpu.VMEM((2, 2, depth + 1, span) + one, F32),
                pltpu.VMEM((8, width), F32), pltpu.VMEM((8, width), F32),
                pltpu.VMEM((depth, width), F32), pltpu.VMEM((depth, width), jnp.int32), pltpu.VMEM((1, reactions), F32),
                pltpu.VMEM((reactions, cells), F32), pltpu.VMEM((reactions, cells + width), F32),
                pltpu.VMEM((2, reactions, cells + width), BF16), pltpu.VMEM((2, reactions, cells), BF16),
                pltpu.VMEM((species, reactions), jnp.int32), pltpu.VMEM((species, reactions), jnp.int32),
                pltpu.VMEM((reactions, 2 * species), BF16), pltpu.VMEM((species, reactions), BF16),
                pltpu.VMEM((reactions, 2 * species), BF16), pltpu.VMEM((species, reactions), BF16),
                pltpu.VMEM((reactions, width), F32),
                dma((2, depth)), dma((5,)),
                dma((2, 2, depth, span)), dma((2, 2, span + 1)), dma((2, 2, depth + 1, span)),
                dma((2, 2, depth + 1, span)), dma((2, 2)), dma((6,)), dma((6,)),
            ],
            compiler_params=pltpu.CompilerParams(collective_id=0, has_side_effects=True, vmem_limit_bytes=48 * 1024 * 1024),
        )(*[pltpu.with_memory_space_constraint(a, pltpu.HBM) for a in (conc, cotangent, courant, direction, rate_const.reshape(1, reactions), orders.T, stoich)])
        return outs[0], outs[1]

    placed = (
        P(None, ("grp", "gx"), ("gy", "row"), None),
        P(None, ("grp", "gx"), ("gy", "row"), None),
        P(("grp", "gy", "row"), None),
        P(("grp", "gy", "row"), None),
        P(),
        P(),
        P(),
    )
    return jax.shard_map(
        shards,
        mesh=mesh,
        in_specs=placed,
        out_specs=(P(None, ("grp", "gx"), ("gy", "row"), None),) * 2,
        check_vma=False,
    )
```

```python
import functools

import jax
import jax.numpy as jnp
from jax import lax
from jax.experimental import pallas as pl
from jax.experimental.pallas import tpu as pltpu
from jax.sharding import PartitionSpec as P

MESH = pl.DeviceIdType.MESH
F32 = jnp.float32
BF16 = jnp.bfloat16
TIME_STEP = 0.1
DIFFUSION = 0.1
HALF_LOG2E = 0.5 * 1.4426950408889634
STAR0, CARRY1, STAR1, CARRY0 = range(4)
DIRECT, RELAY, PAIR, CHAIN = (0, 1, 2, 3), (0, 1, 2, 0), (0, 1, 0, 1), (0, 1, 0, 0)


def plan(kind, nx):
    raw, led = {}, {}
    for q in range(1, nx):
        count = kind[q] if q < len(kind) else 0
        for k in range(1, count + 1):
            raw.setdefault(k, []).append(q)
        if count < q:
            led.setdefault(count + 1, []).append(q)
    return raw, led


def member(q, places):
    found, places = None, sorted(places)
    while places:
        size = 1
        while size < len(places) and places[size] == places[0] + size:
            size += 1
        run = (q >= places[0]) & (q <= places[size - 1])
        found = run if found is None else found | run
        places = places[size:]
    return found


def kernel(
    sizes, kinds, relays, conc_hbm, cot_hbm, cour_hbm, dir_hbm, const_hbm, ord_hbm, sto_hbm, out,
    conc, cot, state, spread, lam, field, sib, mixed, mixed_h, swept, recv, aux_out, aux_in,
    cour_v, dir_v, const_v, rates0, rates1, rates_b, grad_b,
    ord_i, sto_i, ord2, ord_t, sto2, sto, log_k,
    in_sem, tab_sem, send_sem, dsend_sem, recv_sem, lsend_sem, wrecv_sem, esend_sem, erecv_sem,
):
    nx, ngy, nrow = sizes
    depth, species, width = conc.shape
    halo = depth
    reactions = ord_i.shape[1]
    late = [1, 0] if depth > 1 else [0]
    early = [list(range(r, min(r + 2, depth))) for r in range(2, depth, 2)]
    ends = sorted({0, depth - 1})
    inner = list(range(1, depth - 1))
    order = [r for rows in early for r in rows] + late + [halo]
    spots = {STAR0: ends + inner, STAR1: order}
    chunk = min(256, reactions)
    plans = [[plan(kind, nx) for kind in row_kinds] for row_kinds in kinds]
    spans = [[max([0, *raw, *led]) for raw, led in row_plans] for row_plans in plans]

    x = lax.axis_index("gx")
    gy = lax.axis_index("gy")
    row = lax.axis_index("row")
    q_of = [x, nx - 1 - x]
    there = jnp.where(row == 0, gy > 0, gy < ngy - 1)
    across = {"gy": gy + 2 * row - 1, "row": 1 - row}
    beside = {"row": 1 - row}

    def place(r):
        return r + row * (depth - 1 - 2 * r)

    def load(source, target, base):
        return [pltpu.make_async_copy(source.at[:, 0, r, :], target.at[place(r)], in_sem.at[base, r]) for r in range(depth)]

    loads_conc = load(conc_hbm, conc, 0)
    loads_cot = load(cot_hbm, cot, 1)
    tables = [pltpu.make_async_copy(a, b, tab_sem.at[i]) for i, (a, b) in enumerate(
        ((ord_hbm, ord_i), (sto_hbm, sto_i), (const_hbm, const_v), (cour_hbm, cour_v), (dir_hbm, dir_v)))]
    for copy in tables + loads_conc:
        copy.start()

    def inside(target):
        return (target >= 0) & (target < nx)

    own_span = max(max(row_spans) for row_spans in spans)
    halo_span = max(max([0, *row_plans[halo][0]]) for row_plans in plans)
    partners = [(None, beside)]
    for k in range(1, max(own_span, halo_span) + 1):
        for sign in (1, -1):
            partners.append((inside(x + sign * k), {"gx": x + sign * k}))
    partners.append((there, across))
    for k in range(1, halo_span + 1):
        for sign in (1, -1):
            partners.append((there & inside(x + sign * k), {"gx": x + sign * k, **across}))

    def when(condition, action):
        if condition is None:
            action()
        else:
            pl.when(condition)(action)

    barrier = pltpu.get_barrier_semaphore()
    for condition, device in partners:
        when(condition, lambda: pl.semaphore_signal(barrier, inc=1, device_id=device, device_id_type=MESH))

    for copy in loads_cot:
        copy.start()

    def nothing(ref, *index):
        ref[index] = jnp.zeros_like(ref[index])

    for d in range(2):
        missing = {}
        for p in range(2):
            for r in range(depth + 1):
                raw, led = plans[p][r]
                for k in range(1, spans[p][r] + 1):
                    missing.setdefault((r == halo, *sorted(raw.get(k, []) + led.get(k, []))), []).append((p, d, r, k - 1))
        for (outer, *places), slots in missing.items():
            got = member(q_of[d], places)

            @pl.when(jnp.logical_not(got & there if outer else got))
            def _():
                for slot in slots:
                    nothing(recv, *slot)

    @pl.when(jnp.logical_not(there))
    def _():
        nothing(field, STAR0, halo)
        nothing(aux_in, slice(None))
        for p in range(2):
            for d in range(2):
                nothing(mixed_h, p, d)

    for copy in tables:
        copy.wait()

    def pick(ref, r):
        return jnp.where(row == 0, ref[r:r + 1], ref[depth - 1 - r:depth - r])

    courant = [pick(cour_v, r) for r in range(depth)]
    upward = [pick(dir_v, r).astype(F32) for r in range(depth)]
    aux_out[...] = jnp.zeros_like(aux_out)
    aux_out[0:1] = courant[0]
    aux_out[1:2] = upward[0]
    retain = [c / (1.0 + c) for c in courant]
    admit = [1.0 / (1.0 + c) for c in courant]
    rising = [jnp.broadcast_to(u, (species, width)) > 0.5 for u in upward]

    order_float = ord_i[...].astype(F32)
    order_trans = order_float.T.astype(BF16)
    ord2[:, :species] = order_trans
    ord2[:, species:] = order_trans
    stoich_float = sto_i[...].astype(F32)
    sto[...] = stoich_float.astype(BF16)
    log_k[...] = jnp.broadcast_to(jnp.log(const_v[...]) * (2.0 * HALF_LOG2E), (width, reactions)).T
    for copy in loads_conc:
        copy.wait()

    drains = []

    def begin(condition, make):
        when(condition, lambda: make().start())
        drains.append((condition, make))

    def drain():
        for condition, make in drains:
            when(condition, lambda: make().wait_send())
        drains.clear()

    def along(p, d, r, k, source, swept_value):
        return pltpu.make_async_remote_copy(
            src_ref=source, dst_ref=recv.at[p, d, r, k - 1],
            send_sem=(lsend_sem if swept_value else send_sem).at[p, d, r, k - 1], recv_sem=recv_sem.at[p, d, r, k - 1],
            device_id={"gx": x + k * (1 - 2 * d)}, device_id_type=MESH)

    def aslant(p, d, k):
        return pltpu.make_async_remote_copy(
            src_ref=mixed.at[p, d, 0], dst_ref=mixed_h.at[p, d] if k == 0 else recv.at[p, d, halo, k - 1],
            send_sem=dsend_sem.at[p, d, k], recv_sem=wrecv_sem.at[p, d] if k == 0 else recv_sem.at[p, d, halo, k - 1],
            device_id={"gx": x + k * (1 - 2 * d), **across} if k else across, device_id_type=MESH)

    def send_raw(p, r):
        for k in sorted(plans[p][r][0], reverse=True):
            for d in range(2):
                begin(member(q_of[d], [q - k for q in plans[p][r][0][k]]), functools.partial(along, p, d, r, k, mixed.at[p, d, r], False))

    def send_aslant(p):
        for k in sorted(plans[p][halo][0], reverse=True):
            for d in range(2):
                begin(there & member(q_of[d], [q - k for q in plans[p][halo][0][k]]), functools.partial(aslant, p, d, k))
        for d in range(2):
            begin(there, functools.partial(aslant, p, d, 0))

    def arrivals(p, d, r):
        raw, led = plans[p][r]
        if r == halo:
            yield there, aslant(p, d, 0)
        for k in range(1, spans[p][r] + 1):
            for table in (raw, led):
                if k in table:
                    got = member(q_of[d], table[k])
                    yield got & there if r == halo and table is raw else got, along(p, d, r, k, recv.at[p, d, r, k - 1], False)

    def passing(p, r, places=None):
        return [q - k for k, got in plans[p][r][1].items() for q in got if places is None or q - k in places]

    def total(p, d, r):
        value = mixed_h[p, d] if r == halo else mixed[p, d, r]
        carried = None
        for k in range(spans[p][r], 0, -1):
            carried = recv[p, d, r, k - 1] if carried is None else recv[p, d, r, k - 1] + retain[r] * carried
        return value if carried is None else value + retain[r] * carried

    def relay(p, r, places):
        for d in range(2):
            if not passing(p, r, places):
                continue

            @pl.when(member(q_of[d], passing(p, r, places)))
            def _():
                for got, copy in arrivals(p, d, r):
                    pl.when(got)(copy.wait_recv)
                swept[p, d, r] = total(p, d, r)
            for k, got in plans[p][r][1].items():
                senders = [q - k for q in got if q - k in places]
                if senders:
                    begin(member(q_of[d], senders), functools.partial(along, p, d, r, k, swept.at[p, d, r], True))

    def collect(p, r):
        for d in range(2):
            for got, copy in arrivals(p, d, r):
                if passing(p, r):
                    got = got & jnp.logical_not(member(q_of[d], passing(p, r)))
                pl.when(got)(copy.wait_recv)
        ahead, back = total(p, 0, r), total(p, 1, r)
        return jnp.where(rising[r], ahead, back), jnp.where(rising[r], back, ahead)

    def edge_copy(k):
        if k < 4:
            return pltpu.make_async_remote_copy(
                src_ref=field.at[k, depth - 1], dst_ref=sib.at[k], send_sem=esend_sem.at[k], recv_sem=erecv_sem.at[k],
                device_id=beside, device_id_type=MESH)
        source, target = ((field.at[STAR0, 0], field.at[STAR0, halo]), (aux_out, aux_in))[k - 4]
        return pltpu.make_async_remote_copy(
            src_ref=source, dst_ref=target, send_sem=esend_sem.at[k], recv_sem=erecv_sem.at[k],
            device_id=across, device_id_type=MESH)

    def edge_send(k):
        begin(None if k < 4 else there, functools.partial(edge_copy, k))

    def edge_wait(k):
        when(None if k < 4 else there, lambda: edge_copy(k).wait_recv())

    lane = lax.broadcasted_iota(jnp.int32, (species, width), 1)

    def smooth(k, r):
        here = field[k, r]
        below = field[k, halo] if r == 0 else field[k, r - 1]
        above = sib[k] if r == depth - 1 else field[k, r + 1]
        before = jnp.where(lane == 0, 0.0, pltpu.roll(here, 1, 1))
        after = jnp.where(lane == width - 1, 0.0, pltpu.roll(here, width - 1, 1))
        return here + DIFFUSION * (above + below + after + before - 4.0 * here)

    def side(parts):
        return parts[0] if len(parts) == 1 else jnp.concatenate(parts, axis=1)

    def split(value):
        high = value.astype(BF16)
        low = (value - high.astype(F32)).astype(BF16)
        return jnp.concatenate([high, low], axis=0)

    parts = [pl.ds(i, chunk) for i in range(0, reactions, chunk)]

    def keep(target, part, cols, value):
        high = value.astype(BF16)
        target[0, part, cols] = high
        target[1, part, cols] = (value - high.astype(F32)).astype(BF16)

    def gather(table, part, value, so_far):
        high = value.astype(BF16)
        low = (value - high.astype(F32)).astype(BF16)
        small = jnp.dot(table[:, part], low, preferred_element_type=F32)
        both = small + jnp.dot(table[:, part], high, preferred_element_type=F32)
        return both if so_far is None else so_far + both

    def columns(listed, rows):
        return pl.ds(listed.index(rows[0]) * width, len(rows) * width)

    def react(rows, source, rates_ref, k):
        act, cols = split(side([HALF_LOG2E * jnp.log(1.0 + source[r] * source[r]) for r in rows])), columns(spots[k], rows)
        produced = None
        for part in parts:
            exponent = jnp.dot(ord2[part, :], act, preferred_element_type=F32)
            rates = jnp.exp2(exponent + side([log_k[part, :]] * len(rows)))
            rates_ref[part, cols] = rates
            produced = gather(sto, part, rates, produced)
        for i, r in enumerate(rows):
            value = source[r] + TIME_STEP * produced[:, i * width:(i + 1) * width]
            field[k, r] = jnp.where(there, value, 0.0) if r == halo else value

    def react_back(rows, cells, rates_ref, k, put):
        cols = columns(order, rows)
        push = split(side([spread[r] for r in rows]))
        summed = None
        for part in parts:
            pulled = jnp.dot(sto2[part, :], push, preferred_element_type=F32)
            summed = gather(ord_t, part, side([rates_ref[part, columns(spots[k], [r])] for r in rows]) * pulled, summed)
        for i, r in enumerate(rows):
            c = cells[r]
            put(r, spread[r] + TIME_STEP * c / (1.0 + c * c) * summed[:, i * width:(i + 1) * width])

    def mix(p, k, r, back):
        ahead = admit[r] * smooth(k, r)
        mixed[p, 0, r] = jnp.where(rising[r], ahead, back[r])
        mixed[p, 1, r] = jnp.where(rising[r], back[r], ahead)

    def put(target, r, value):
        for side_row in range(2):
            @pl.when(row == side_row)
            def _():
                out[target, :, 0, depth - 1 - r if side_row else r, :] = value

    def put_lam(r, value):
        lam[r] = value

    def put_out(r, value):
        put(1, r, value)

    last = depth - 1

    react(ends, conc, rates0, STAR0)
    pl.semaphore_wait(barrier, sum(1 if c is None else jnp.where(c, 1, 0) for c, _ in partners))
    edge_send(4)
    edge_send(STAR0)
    edge_send(5)
    for i in range(0, len(inner), 2):
        react(inner[i:i + 2], conc, rates0, STAR0)
    for copy in loads_cot:
        copy.wait()
    edge_wait(STAR0)
    for r in range(last, 0, -1):
        mix(0, STAR0, r, cot)
        send_raw(0, r)
    ord_t[...] = ord_i[...].astype(F32).astype(BF16)
    stoich_trans = sto_i[...].astype(F32).T.astype(BF16)
    sto2[:, :species] = stoich_trans
    sto2[:, species:] = stoich_trans
    edge_wait(4)
    mix(0, STAR0, 0, cot)
    send_aslant(0)
    send_raw(0, 0)
    edge_wait(5)
    retain.append(aux_in[0:1] / (1.0 + aux_in[0:1]))
    admit.append(1.0 / (1.0 + aux_in[0:1]))
    rising.append(jnp.broadcast_to(aux_in[1:2], (species, width)) > 0.5)
    for r, places in relays[0]:
        relay(0, r, places)

    def gain(r):
        ahead, back = collect(0, r)
        state[r] = ahead
        field[CARRY1, r] = admit[r] * back

    for rows in early:
        for r in rows:
            gain(r)
        if last in rows:
            edge_send(CARRY1)
        react(rows, state, rates1, STAR1)
    if last > 1:
        edge_send(STAR1)
    if depth > 1:
        gain(1)
        if last == 1:
            edge_send(CARRY1)
        react([1], state, rates1, STAR1)
        if last == 1:
            edge_send(STAR1)
    for rows in early:
        for r in rows:
            if r == last:
                edge_wait(CARRY1)
            spread[r] = smooth(CARRY1, r)
        react_back(rows, state, rates1, STAR1, put_lam)
    marked = len(drains)
    for rows in early:
        for r in rows:
            if r == last:
                edge_wait(STAR1)
            mix(1, STAR1, r, lam)
            send_raw(1, r)
    gain(0)
    gain(halo)
    if last == 0:
        edge_send(CARRY1)
    react([0, halo], state, rates1, STAR1)
    if last == 0:
        edge_send(STAR1)
    for r in late:
        if r == last:
            edge_wait(CARRY1)
        spread[r] = smooth(CARRY1, r)
    react_back(late, state, rates1, STAR1, put_lam)
    for r in late:
        if r == last:
            edge_wait(STAR1)
        mix(1, STAR1, r, lam)
        if r == 0:
            send_aslant(1)
        send_raw(1, r)
    for r, places in relays[1]:
        relay(1, r, places)

    drain_late = drains[marked:]
    del drains[marked:]
    drain()
    drains.extend(drain_late)

    def finish(r):
        ahead, back = collect(1, r)
        if r != halo:
            put(0, r, ahead)
        field[CARRY0, r] = admit[r] * back
        if r == last:
            edge_send(CARRY0)

    for rows in early:
        for r in rows:
            finish(r)
    for r in late:
        if r:
            finish(r)
    for rows in early:
        for r in rows:
            if r == last:
                edge_wait(CARRY0)
            spread[r] = smooth(CARRY0, r)
        react_back(rows, conc, rates0, STAR0, put_out)
    drain()
    finish(0)
    finish(halo)
    for r in late:
        if r == last:
            edge_wait(CARRY0)
        spread[r] = smooth(CARRY0, r)
    react_back(late, conc, rates0, STAR0, put_out)

    drain()


def solution(mesh):
    sizes = (mesh.shape["gx"], mesh.shape["gy"], mesh.shape["row"])
    assert sizes[2] == 2

    def shards(conc, cotangent, courant, direction, rate_const, orders, stoich):
        species, slabs, depth, width = conc.shape
        reactions = orders.shape[0]
        assert slabs == 1
        kinds, relays = [[CHAIN] * (depth + 1)] * 2, [[(r, range(sizes[0])) for r in range(depth + 1)]] * 2
        if sizes[0] <= 4 and depth == 4:
            kinds, relays = [[PAIR,RELAY,PAIR,PAIR,PAIR],[PAIR,PAIR,PAIR,PAIR,RELAY]], [[(r, [q]) for r, q in steps] for steps in [[(3, 1), (2, 1), (1, 2), (4, 1), (0, 1)], [(2, 1), (3, 1), (1, 1), (4, 2), (0, 1)]]]
        span = max(max([0, *raw, *led]) for row_kinds in kinds for raw, led in (plan(kind, sizes[0]) for kind in row_kinds)) or 1
        block = (depth, species, width)
        more = (depth + 1, species, width)
        one = (species, width)
        hbm = pl.BlockSpec(memory_space=pltpu.HBM)
        vmem = pl.BlockSpec(memory_space=pltpu.VMEM)
        cells = depth * width
        dma = pltpu.SemaphoreType.DMA
        outs = pl.pallas_call(
            functools.partial(kernel, sizes, kinds, relays),
            name="flame_adjoint",
            out_shape=jax.ShapeDtypeStruct((2, species, 1, depth, width), F32),
            in_specs=[hbm] * 7,
            out_specs=vmem,
            scratch_shapes=[
                pltpu.VMEM(block, F32), pltpu.VMEM(block, F32), pltpu.VMEM(more, F32), pltpu.VMEM(block, F32), pltpu.VMEM(block, F32),
                pltpu.VMEM((4,) + more, F32), pltpu.VMEM((4,) + one, F32),
                pltpu.VMEM((2, 2) + block, F32), pltpu.VMEM((2, 2) + one, F32), pltpu.VMEM((2, 2) + more, F32),
                pltpu.VMEM((2, 2, depth + 1, span) + one, F32),
                pltpu.VMEM((8, width), F32), pltpu.VMEM((8, width), F32),
                pltpu.VMEM((depth, width), F32), pltpu.VMEM((depth, width), jnp.int32), pltpu.VMEM((1, reactions), F32),
                pltpu.VMEM((reactions, cells), F32), pltpu.VMEM((reactions, cells + width), F32),
                pltpu.VMEM((2, reactions, cells + width), BF16), pltpu.VMEM((2, reactions, cells), BF16),
                pltpu.VMEM((species, reactions), jnp.int32), pltpu.VMEM((species, reactions), jnp.int32),
                pltpu.VMEM((reactions, 2 * species), BF16), pltpu.VMEM((species, reactions), BF16),
                pltpu.VMEM((reactions, 2 * species), BF16), pltpu.VMEM((species, reactions), BF16),
                pltpu.VMEM((reactions, width), F32),
                dma((2, depth)), dma((5,)),
                dma((2, 2, depth, span)), dma((2, 2, span + 1)), dma((2, 2, depth + 1, span)),
                dma((2, 2, depth + 1, span)), dma((2, 2)), dma((6,)), dma((6,)),
            ],
            compiler_params=pltpu.CompilerParams(collective_id=0, has_side_effects=True, vmem_limit_bytes=48 * 1024 * 1024),
        )(*[pltpu.with_memory_space_constraint(a, pltpu.HBM) for a in (conc, cotangent, courant, direction, rate_const.reshape(1, reactions), orders.T, stoich)])
        return outs[0], outs[1]

    placed = (
        P(None, ("grp", "gx"), ("gy", "row"), None),
        P(None, ("grp", "gx"), ("gy", "row"), None),
        P(("grp", "gy", "row"), None),
        P(("grp", "gy", "row"), None),
        P(),
        P(),
        P(),
    )
    return jax.shard_map(
        shards,
        mesh=mesh,
        in_specs=placed,
        out_specs=(P(None, ("grp", "gx"), ("gy", "row"), None),) * 2,
        check_vma=False,
    )
```
